256 devices in a mesh: seq: 32 (over y, x, core), head: 8 (over z).
Axes of the slice: x: 4, y: 4, z: 8, core: 2. Of those that a mesh axis runs over, the one named last changes fastest.
Arguments:
- tokens: bfloat16 [32768, 2048], P(('seq', 'head')), may hold values from -6 to 6
- w_qkv: bfloat16 [2048, 3, 2048], P(None, None, 'head'), may hold values from -0.125 to 0.125
- w_beta: bfloat16 [2048, 16], P(None, 'head'), may hold values from -0.125 to 0.125
- beta_bias: float32 [16], P('head'), may hold values from -8 to 2
- w_out: bfloat16 [2048, 2048], P('head'), may hold values from -0.125 to 0.125
Outputs:
- mixed: bfloat16 [32768, 2048], P(('seq', 'head'))
The draws below stay inside these ranges and needn't reach their ends.
All inputs are finite; a program needn't handle non-finite values.
Results may differ from the reference program's by a relative error of at most 0.015.
Values may be sent and summed in bfloat16 or wider, within the bound.
A program may use at most 64 MiB of HBM per device.

```python
import jax
import jax.numpy as jnp
from jax import lax

D = 2048
H = 16
DK = 128
C = 64
TOKENS = 32768
N_HEAD = 8


def shard_levels(key, shape, shards, least, largest):
    level = 1.0
    for axis_at, parts in shards:
        draws = jax.random.uniform(jax.random.fold_in(jax.random.fold_in(key, 6), axis_at), (parts,), jnp.float32, least / len(shards), largest / len(shards))
        level = level * jnp.repeat(jnp.exp(draws), shape[axis_at] // parts).reshape((-1,) + (1,) * (len(shape) - 1 - axis_at))
    return level


def bell_draw(rng, dims, width, limit, cuts=(), held_as=jnp.bfloat16):
    loudness = shard_levels(rng, dims, cuts, -0.22, 0.18) if cuts else 1.0
    result = jax.random.normal(rng, dims, jnp.float32) * width * loudness
    return jnp.minimum(jnp.maximum(result, -limit), limit).astype(held_as)


def setup_inputs(seed: int = 0) -> dict:
    keys = jax.random.split(jax.random.key(seed), 6)
    return {
        "tokens": bell_draw(keys[0], (TOKENS, D), 1.0, 6.0, ((0, 256),)),
        "w_qkv": bell_draw(keys[1], (D, 3, H * DK), D ** -0.5, 0.125, ((2, 8),)),
        "w_beta": bell_draw(keys[2], (D, H), D ** -0.5, 0.125, ((1, 8),)),
        "beta_bias": jnp.clip(-8.0 + 10.0 * jax.random.uniform(keys[3], (H,), jnp.float32) ** shard_levels(keys[3], (H,), ((0, 8),), -0.2, 0.2), -8.0, 2.0),
        "w_out": bell_draw(keys[4], (H * DK, D), (H * DK) ** -0.5, 0.125, ((0, 8),)),
    }


epsilon = 1e-06

def unit_norm(values):
    return values * lax.rsqrt(lax.optimization_barrier(jnp.sum(values * values, -1, keepdims=True)) + epsilon)

def prepare(queries, key_rows, value_rows, strength):
    highest = lax.Precision.HIGHEST
    size_k = key_rows.shape[-1]
    similar = jnp.einsum('...id,...jd->...ij', key_rows, key_rows, precision=highest)
    system = jnp.eye(C, dtype=jnp.float32) + jnp.tril(similar * strength[..., :, None], -1)
    weighted = jnp.concatenate([strength[..., None] * key_rows, strength[..., None] * value_rows], -1)
    solved = jax.scipy.linalg.solve_triangular(system, weighted, lower=True, unit_diagonal=True)
    w_fac = solved[..., :size_k]
    u_fac = solved[..., size_k:]
    masked = jnp.tril(jnp.einsum('...id,...jd->...ij', queries, key_rows, precision=highest))
    q_eff = queries - jnp.einsum('...ij,...jd->...id', masked, w_fac, precision=highest)
    return (w_fac, u_fac, masked, q_eff)

def reference(tokens, w_qkv, w_beta, beta_bias, w_out):
    highest = lax.Precision.HIGHEST
    float_tokens = tokens.astype(jnp.float32)
    normed = (float_tokens * lax.rsqrt(lax.optimization_barrier(jnp.mean(float_tokens * float_tokens, -1, keepdims=True)) + epsilon)).astype(jnp.bfloat16)
    projected = jnp.dot(normed.astype(jnp.float32), w_qkv.reshape(D, 3 * H * DK).astype(jnp.float32), preferred_element_type=jnp.float32).reshape(TOKENS, 3, H, DK)
    queries = unit_norm(jax.nn.silu(projected[:, 0]))
    key_rows = unit_norm(jax.nn.silu(projected[:, 1]))
    value_rows = jax.nn.silu(projected[:, 2])
    strength = jax.nn.sigmoid(jnp.dot(normed.astype(jnp.float32), w_beta.astype(jnp.float32), preferred_element_type=jnp.float32) + beta_bias)
    block_count = TOKENS // C

    def blocks(values):
        return values.reshape(block_count, C, H, -1).transpose(0, 2, 1, 3)
    key_blocks = blocks(key_rows)
    w_fac, u_fac, masked, q_eff = prepare(blocks(queries), key_blocks, blocks(value_rows), strength.reshape(block_count, C, H).transpose(0, 2, 1))

    def advance(state, pieces):
        w_blk, u_blk, m_blk, qe_blk, k_blk = pieces
        local_out = jnp.einsum('hcj,hvj->hcv', qe_blk, state, precision=highest) + jnp.einsum('hcd,hdv->hcv', m_blk, u_blk, precision=highest)
        state_w = jnp.einsum('hvj,hcj->hvc', state, w_blk, precision=highest)
        change = u_blk.transpose(0, 2, 1) - state_w
        return (state + jnp.einsum('hvc,hcd->hvd', change, k_blk, precision=highest), local_out)
    start_state = jnp.zeros((H, DK, DK), jnp.float32)
    _, outputs = lax.scan(advance, start_state, (w_fac, u_fac, masked, q_eff, key_blocks))
    outputs = outputs.transpose(0, 2, 1, 3).reshape(TOKENS, H, DK)
    outputs = outputs * lax.rsqrt(lax.optimization_barrier(jnp.mean(outputs * outputs, -1, keepdims=True)) + epsilon)
    flat_out = outputs.reshape(TOKENS, H * DK).astype(jnp.bfloat16)
    group_width = H // N_HEAD * DK

    def add_group(running, group_index):
        begin = (group_index * group_width).astype(jnp.int32)
        piece = lax.dynamic_slice_in_dim(flat_out, begin, group_width, 1)
        weight_part = lax.dynamic_slice_in_dim(w_out, begin, group_width, 0)
        term = jnp.dot(piece.astype(jnp.float32), weight_part.astype(jnp.float32), preferred_element_type=jnp.float32).astype(jnp.bfloat16)
        term = lax.optimization_barrier(term)
        return (running + term.astype(jnp.float32), None)
    running, _ = lax.scan(add_group, jnp.zeros((TOKENS, D), jnp.float32), jnp.arange(N_HEAD, dtype=jnp.int32))
    return running.astype(jnp.bfloat16)
```

```python
import jax
import jax.numpy as jnp
from jax import lax
from jax.experimental import pallas as pl
from jax.experimental.pallas import tpu as pltpu
from jax.sharding import PartitionSpec as P

F32 = jnp.float32
BF16 = jnp.bfloat16
MESH = pl.DeviceIdType.MESH
EPS = 1e-6
NZ = 8
NX = 4
NY = 4
NC = 2
C = 64
DK = 128
D = 2048

NN = (((1,), (0,)), ((), ()))
NT = (((1,), (1,)), ((), ()))
TN = (((0,), (0,)), ((), ()))


def halves(a):
    hi = a.astype(BF16)
    lo = (a - hi.astype(F32)).astype(BF16)
    return hi, lo


def dot3(a, b, dims=NN):
    ca = dims[0][0][0]
    cb = dims[0][1][0]
    ah, al = halves(a)
    bh, bl = halves(b)
    return lax.dot_general(
        jnp.concatenate([ah, al, ah], ca),
        jnp.concatenate([bh, bh, bl], cb),
        dims,
        preferred_element_type=F32,
    )


def compose(first, second):
    return first + dot3(first, second[:DK]) + second


def kernel(
    tok_ref,
    w3_hbm,
    wb_ref,
    bias_ref,
    wo_hbm,
    out_ref,
    g,
    w3,
    wbt,
    wo,
    qe,
    mu,
    db,
    tot,
    lv,
    xs,
    xr,
    sin,
    ss,
    osend,
    fbuf,
    acc,
    lsem,
    agr_s,
    agr_r,
    agl_s,
    agl_r,
    wz_s,
    wz_r,
    w1_s,
    w1_r,
    w2_s,
    w2_r,
    wc_s,
    wc_r,
    sc_s,
    sc_r,
    a2_s,
    a2_r,
):
    s = lax.axis_index("seq")
    z = lax.axis_index("head")
    c = lax.rem(s, NC)
    x = lax.rem(s // NC, NX)
    y = s // (NC * NX)

    def at_z(d):
        return (s, lax.rem(z + d, NZ))

    def at_x(d):
        return ((y * NX + lax.rem(x + d, NX)) * NC + c, z)

    def at_y(d):
        return ((lax.rem(y + d, NY) * NX + x) * NC + c, z)

    partner = ((y * NX + x) * NC + (1 - c), z)

    peers = [at_z(d) for d in range(1, NZ)]
    peers += [at_x(d) for d in range(1, NX)]
    peers += [at_y(d) for d in range(1, NY)]
    peers += [partner]
    barrier = pltpu.get_barrier_semaphore()
    for p in peers:
        pl.semaphore_signal(barrier, inc=1, device_id=p, device_id_type=MESH)

    cp_w3 = pltpu.make_async_copy(w3_hbm, w3, lsem.at[0])
    cp_w3.start()
    cp_wo = pltpu.make_async_copy(
        wo_hbm.at[y, x, :, pl.ds(pl.multiple_of(c * 1024, 1024), 1024)],
        wo.at[c, z, y, x],
        lsem.at[1],
    )
    cp_wo.start()

    for j in range(2):
        t = tok_ref[j * C : (j + 1) * C, :].astype(F32)
        ms = jnp.mean(t * t, -1, keepdims=True)
        g[z, j] = (t * lax.rsqrt(ms + EPS)).astype(BF16)

    pl.semaphore_wait(barrier, len(peers))

    def remote(src, dst, ssem, rsem, dev):
        return pltpu.make_async_remote_copy(
            src_ref=src, dst_ref=dst, send_sem=ssem, recv_sem=rsem,
            device_id=dev, device_id_type=MESH,
        )

    def right(i):
        o = lax.rem(z + NZ - i // 2, NZ)
        ref = g.at[o, lax.rem(i, 2)]
        return remote(ref, ref, agr_s.at[i], agr_r.at[i], at_z(1))

    def left(i):
        o = lax.rem(z + i // 2, NZ)
        ref = g.at[o, jnp.where(i == 6, 1, lax.rem(i, 2))]
        return remote(ref, ref, agl_s.at[i], agl_r.at[i], at_z(NZ - 1))

    for i in range(2):
        right(jnp.int32(i)).start()
        left(jnp.int32(i)).start()

    cp_wo.wait()

    def wz(d):
        ref = wo.at[c, z, y, x]
        return remote(ref, ref, wz_s.at[d - 1], wz_r.at[d - 1], at_z(d))

    def w1x(d):
        ref = wo.at[c, pl.ds(0, 4), y, x]
        return remote(ref, ref, w1_s.at[d - 1], w1_r.at[d - 1], at_x(d))

    def w1y(d):
        ref = wo.at[c, pl.ds(4, 4), y, x]
        return remote(ref, ref, w1_s.at[d + 2], w1_r.at[d + 2], at_y(d))

    def w2y(d):
        ref = wo.at[c, pl.ds(0, 4), y]
        return remote(ref, ref, w2_s.at[d - 1], w2_r.at[d - 1], at_y(d))

    def w2x(d):
        ref = wo.at[c, pl.ds(4, 4), :, x]
        return remote(ref, ref, w2_s.at[d + 2], w2_r.at[d + 2], at_x(d))

    for d in range(1, NZ):
        wz(d).start()

    for h in range(2):
        row = jnp.broadcast_to(wb_ref[h : h + 1, :].astype(F32), (DK, D))
        wbt[:, h * DK : (h + 1) * DK] = row.T.astype(BF16)
    cp_w3.wait()

    ri = lax.broadcasted_iota(jnp.int32, (DK, DK), 0)
    ci = lax.broadcasted_iota(jnp.int32, (DK, DK), 1)
    same = (ri // C) == (ci // C)
    strict = same & (ri > ci)
    lower = same & (ri >= ci)
    eye = jnp.where(ri == ci, 1.0, 0.0).astype(F32)

    def level_mask(b):
        return (
            ((ri // (2 * b)) == (ci // (2 * b)))
            & (lax.rem(ri // b, 2) == 1)
            & (lax.rem(ci // b, 2) == 0)
        )

    def unit(v):
        return v * lax.rsqrt(jnp.sum(v * v, -1, keepdims=True) + EPS)

    def silu(v):
        return v / (1.0 + jnp.exp(-v))

    def joint(pieces):
        rows = jnp.concatenate([g[o, j] for o, j in pieces], 0)
        proj = [
            jnp.dot(rows, w3[p], preferred_element_type=F32) for p in range(3)
        ]
        pre = jnp.dot(rows, wbt[...], preferred_element_type=F32)
        qs = silu(proj[0])
        ks = silu(proj[1])
        vs = silu(proj[2])
        qh = [unit(qs[:, h * DK : (h + 1) * DK]) for h in range(2)]
        kh = [unit(ks[:, h * DK : (h + 1) * DK]) for h in range(2)]
        vh = [vs[:, h * DK : (h + 1) * DK] for h in range(2)]
        bh = [
            1.0 / (1.0 + jnp.exp(-(pre[:, h * DK : (h + 1) * DK] + bias_ref[h])))
            for h in range(2)
        ]
        for a, (o, j) in enumerate(pieces):
            part = slice(a * C, (a + 1) * C)
            q = jnp.concatenate([qh[0][part], qh[1][part]], 0)
            k = jnp.concatenate([kh[0][part], kh[1][part]], 0)
            v = jnp.concatenate([vh[0][part], vh[1][part]], 0)
            b = jnp.concatenate([bh[0][part], bh[1][part]], 0)
            both = dot3(jnp.concatenate([k, q], 0), k, NT)
            low = jnp.where(strict, both[:DK] * b, 0.0)
            masked = jnp.where(lower, both[DK:], 0.0)
            inv = eye - jnp.where(level_mask(1), low, 0.0)
            for size in (2, 4, 8, 16, 32):
                part_low = jnp.where(level_mask(size), low, 0.0)
                inv = inv - dot3(dot3(inv, part_low), inv)
            wu = dot3(inv, jnp.concatenate([b * k, b * v], 1))
            mwu = dot3(masked, wu)
            blk = 2 * o + j
            for h in range(2):
                hp = slice(h * C, (h + 1) * C)
                qe[h, blk] = q[hp] - mwu[hp, :DK]
                mu[h, blk] = mwu[hp, DK:]
                pair = dot3(wu[hp], k[hp], TN)
                db[h, blk, :DK] = -pair[:DK]
                db[h, blk, DK:] = pair[DK:]

    def step(t, carry):
        i = t - 1

        @pl.when(t >= 1)
        def _():
            right(i).wait_recv()

            @pl.when(i <= 4)
            def _():
                right(i + 2).start()

            left(i).wait_recv()

            @pl.when(i <= 3)
            def _():
                left(i + 2).start()

            @pl.when(i == 5)
            def _():
                left(i + 1).start()

        @pl.when(t == 1)
        def _():
            for d in range(1, NZ):
                wz(d).wait_recv()
            for d in range(1, NX):
                w1x(d).start()
                w1y(d).start()

        @pl.when(t == 3)
        def _():
            for d in range(1, NX):
                w1x(d).wait_recv()
                w1y(d).wait_recv()
            for d in range(1, NX):
                w2y(d).start()
                w2x(d).start()

        hop = (i + 2) // 2
        mid = jnp.logical_and(t >= 1, t <= 6)
        hop = jnp.where(t == 0, 0, hop)
        ja = jnp.where(mid, lax.rem(t + 1, 2), 0)
        jb = jnp.where(mid, lax.rem(t + 1, 2), 1)
        oa = lax.rem(z + NZ - hop, NZ)
        ob = lax.rem(z + hop, NZ)
        joint([(oa, ja), (ob, jb)])
        return carry

    lax.fori_loop(0, 8, step, 0)

    for d in range(1, NX):
        w2y(d).wait_recv()
        w2x(d).wait_recv()

    def fold_in(b, carry):
        nxt = []
        for h in range(2):
            here = db[h, b]
            db[h, b] = carry[h]
            nxt.append(compose(carry[h], here))
        return tuple(nxt)

    zero = jnp.zeros((2 * DK, DK), F32)
    ends = lax.fori_loop(0, 2 * NZ, fold_in, (zero, zero))
    for h in range(2):
        tot[h] = ends[h]

    def core_swap():
        return remote(tot.at[1 - c], lv.at[c], sc_s.at[0], sc_r.at[0], partner)

    core_swap().start()
    lv[c] = tot[c]

    def fold_queries(first, last):
        def one(b, carry):
            for h in range(2):
                q = qe[h, b]
                both = dot3(q, db[h, b], NT)
                qe[h, b] = q + both[:, :DK]
                mu[h, b] = mu[h, b] + both[:, DK:]
            return carry

        lax.fori_loop(first, last, one, 0)

    core_swap().wait_recv()

    wc = remote(wo.at[c], wo.at[c], wc_s.at[0], wc_r.at[0], partner)
    wc.start()

    group = compose(lv[0], lv[1])
    before = jnp.zeros((2 * DK, DK), F32)
    xp = jnp.where(lax.rem(x, 2) == 0, 1, NX - 1)
    yp = jnp.where(lax.rem(y, 2) == 0, 1, NY - 1)
    xq = lax.rem(2 * NX - 1 - 2 * x, NX)
    yq = lax.rem(2 * NY - 1 - 2 * y, NY)
    levels = [
        (at_x(xp), lax.rem(x, 2) == 0),
        (at_x(xq), x < 2),
        (at_y(yp), lax.rem(y, 2) == 0),
        (at_y(yq), y < 2),
    ]
    sends = []
    for n, (dev, is_low) in enumerate(levels):
        xs[n] = group.astype(BF16)
        cp = remote(xs.at[n], xr.at[n], sc_s.at[n + 1], sc_r.at[n + 1], dev)
        cp.start()
        sends.append(cp)
        fold_queries(4 * n, 4 * n + 4)
        cp.wait_recv()
        other = xr[n].astype(F32)
        low = jnp.broadcast_to(is_low.astype(jnp.int32), (2 * DK, DK)) > 0
        if n < 3:
            group = compose(jnp.where(low, group, other), jnp.where(low, other, group))
        before = jnp.where(low, before, compose(other, before))

    s0 = before[DK:]
    first = lv[0]
    s1 = s0 + dot3(s0, first[:DK]) + first[DK:]
    zero_core = jnp.broadcast_to(c, (DK, DK)) == 0
    ss[...] = jnp.where(zero_core, s1, s0)
    give = remote(ss, sin.at[c], sc_s.at[5], sc_r.at[5], partner)
    give.start()
    sin[c] = jnp.where(zero_core, s0, s1)
    give.wait_recv()

    def a2a(d, o):
        return remote(osend.at[o], fbuf.at[z], a2_s.at[d - 1], a2_r.at[d - 1], (s, o))

    def emit(i, carry):
        d = jnp.where(lax.rem(i, 2) == 1, 4 - (i + 1) // 2, 4 + i // 2)
        o = lax.rem(z + d, NZ)
        cols = []
        for h in range(2):
            q = jnp.concatenate([qe[h, 2 * o], qe[h, 2 * o + 1]], 0)
            m = jnp.concatenate([mu[h, 2 * o], mu[h, 2 * o + 1]], 0)
            full = m + dot3(q, sin[h], NT)
            ms = jnp.mean(full * full, -1, keepdims=True)
            cols.append((full * lax.rsqrt(ms + EPS)).astype(BF16))
        rows = jnp.concatenate(cols, 1)

        @pl.when(i < 7)
        def _():
            osend[o] = rows
            a2a(d, o).start()

        @pl.when(i == 7)
        def _():
            fbuf[z] = rows

        return carry

    lax.fori_loop(0, NZ, emit, 0)

    wc.wait_recv()

    def finish(i, carry):
        d = jnp.where(lax.rem(i, 2) == 1, (i + 1) // 2, lax.rem(NZ - i // 2, NZ))
        src = lax.rem(z + NZ - d, NZ)

        @pl.when(i >= 1)
        def _():
            remote(
                osend.at[src], fbuf.at[src], a2_s.at[d - 1], a2_r.at[d - 1], (s, src)
            ).wait_recv()

        rows = fbuf[src]
        for half in range(2):
            w = wo[half, src].reshape(2 * DK, 1024)
            term = jnp.dot(rows, w, preferred_element_type=F32)
            cols = slice(half * 1024, (half + 1) * 1024)

            @pl.when(i == 0)
            def _():
                acc[:, cols] = term

            @pl.when(i >= 1)
            def _():
                acc[:, cols] = acc[:, cols] + term

        return carry

    lax.fori_loop(0, NZ, finish, 0)
    out_ref[...] = acc[...].astype(BF16)

    for i in range(7):
        right(jnp.int32(i)).wait_send()
        left(jnp.int32(i)).wait_send()
    for d in range(1, NZ):
        wz(d).wait_send()
        a2a(d, lax.rem(z + d, NZ)).wait_send()
    for d in range(1, NX):
        w1x(d).wait_send()
        w1y(d).wait_send()
        w2x(d).wait_send()
        w2y(d).wait_send()
    wc.wait_send()
    core_swap().wait_send()
    for cp in sends:
        cp.wait_send()
    give.wait_send()


def body(tokens, w_qkv, w_beta, beta_bias, w_out):
    w3 = jnp.transpose(w_qkv, (1, 0, 2))
    wb = jnp.transpose(w_beta, (1, 0))
    wo = w_out.reshape(NY, NX, 16, D)
    vmem = pl.BlockSpec(memory_space=pltpu.VMEM)
    hbm = pl.BlockSpec(memory_space=pl.ANY)
    smem = pl.BlockSpec(memory_space=pltpu.SMEM)
    dma = pltpu.SemaphoreType.DMA
    return pl.pallas_call(
        kernel,
        out_shape=jax.ShapeDtypeStruct((2 * C, D), BF16),
        in_specs=[vmem, hbm, vmem, smem, hbm],
        out_specs=vmem,
        scratch_shapes=[
            pltpu.VMEM((NZ, 2, C, D), BF16),
            pltpu.VMEM((3, D, 2 * DK), BF16),
            pltpu.VMEM((D, 2 * DK), BF16),
            pltpu.VMEM((2, NZ, NY, NX, 16, 1024), BF16),
            pltpu.VMEM((2, 16, C, DK), F32),
            pltpu.VMEM((2, 16, C, DK), F32),
            pltpu.VMEM((2, 16, 2 * DK, DK), F32),
            pltpu.VMEM((2, 2 * DK, DK), F32),
            pltpu.VMEM((2, 2 * DK, DK), F32),
            pltpu.VMEM((4, 2 * DK, DK), BF16),
            pltpu.VMEM((4, 2 * DK, DK), BF16),
            pltpu.VMEM((2, DK, DK), F32),
            pltpu.VMEM((DK, DK), F32),
            pltpu.VMEM((NZ, 2 * C, 2 * DK), BF16),
            pltpu.VMEM((NZ, 2 * C, 2 * DK), BF16),
            pltpu.VMEM((2 * C, D), F32),
            dma((2,)),
            dma((7,)),
            dma((7,)),
            dma((7,)),
            dma((7,)),
            dma((7,)),
            dma((7,)),
            dma((6,)),
            dma((6,)),
            dma((6,)),
            dma((6,)),
            dma((1,)),
            dma((1,)),
            dma((6,)),
            dma((6,)),
            dma((7,)),
            dma((7,)),
        ],
        compiler_params=pltpu.CompilerParams(
            collective_id=0, has_side_effects=True, vmem_limit_bytes=60 * 1024 * 1024
        ),
        name="delta_layer",
    )(tokens, w3, wb, beta_bias, wo)


def solution(mesh):
    return jax.shard_map(
        body,
        mesh=mesh,
        in_specs=(
            P(("seq", "head"), None),
            P(None, None, "head"),
            P(None, "head"),
            P("head"),
            P("head", None),
        ),
        out_specs=P(("seq", "head"), None),
        check_vma=False,
    )
```

```python
import jax
import jax.numpy as jnp
from jax import lax
from jax.experimental import pallas as pl
from jax.experimental.pallas import tpu as pltpu
from jax.sharding import PartitionSpec as P

F32 = jnp.float32
BF16 = jnp.bfloat16
MESH = pl.DeviceIdType.MESH
EPS = 1e-6
NZ = 8
NX = 4
NY = 4
NC = 2
C = 64
DK = 128
D = 2048

NN = (((1,), (0,)), ((), ()))
NT = (((1,), (1,)), ((), ()))
TN = (((0,), (0,)), ((), ()))


def halves(a):
    hi = a.astype(BF16)
    lo = (a - hi.astype(F32)).astype(BF16)
    return hi, lo


def dot3(a, b, dims=NN):
    ca = dims[0][0][0]
    cb = dims[0][1][0]
    ah, al = halves(a)
    bh, bl = halves(b)
    return lax.dot_general(
        jnp.concatenate([ah, al, ah], ca),
        jnp.concatenate([bh, bh, bl], cb),
        dims,
        preferred_element_type=F32,
    )


def dot1(a, b, dims=NN):
    return lax.dot_general(
        a.astype(BF16), b.astype(BF16), dims, preferred_element_type=F32
    )


def compose(first, second):
    return first + dot3(first, second[:DK]) + second


def kernel(
    tok_ref,
    w3_hbm,
    wb_ref,
    bias_ref,
    wo_hbm,
    out_ref,
    g,
    w3,
    wbt,
    wo,
    qe,
    mu,
    db,
    ct,
    ends,
    tot,
    lv,
    xs,
    xr,
    ys,
    yr,
    eb,
    es,
    sf,
    osend,
    fbuf,
    acc,
    lsem,
    agr_s,
    agr_r,
    agl_s,
    agl_r,
    wzr_s,
    wzr_r,
    wzl_s,
    wzl_r,
    w1_s,
    w1_r,
    w2_s,
    w2_r,
    wc_s,
    wc_r,
    sc_s,
    sc_r,
    a2_s,
    a2_r,
):
    s = lax.axis_index("seq")
    z = lax.axis_index("head")
    c = lax.rem(s, NC)
    x = lax.rem(s // NC, NX)
    y = s // (NC * NX)

    def at_z(d):
        return (s, lax.rem(z + d, NZ))

    def at_x(d):
        return ((y * NX + lax.rem(x + d, NX)) * NC + c, z)

    def at_y(d):
        return ((lax.rem(y + d, NY) * NX + x) * NC + c, z)

    partner = ((y * NX + x) * NC + (1 - c), z)

    peers = [at_z(1), at_z(NZ - 1)]
    peers += [at_x(d) for d in range(1, NX)]
    peers += [at_y(d) for d in range(1, NY)]
    peers += [partner]
    barrier = pltpu.get_barrier_semaphore()
    for p in peers:
        pl.semaphore_signal(barrier, inc=1, device_id=p, device_id_type=MESH)

    cp_w3 = pltpu.make_async_copy(w3_hbm, w3, lsem.at[0])
    cp_w3.start()
    cp_wo = [
        pltpu.make_async_copy(
            wo_hbm.at[:, :, :, pl.ds(q * 1024, 1024)], wo.at[q, z], lsem.at[1 + q]
        )
        for q in range(NC)
    ]
    for cp in cp_wo:
        cp.start()

    for j in range(2):
        t = tok_ref[j * C : (j + 1) * C, :].astype(F32)
        ms = jnp.mean(t * t, -1, keepdims=True)
        g[z, j] = (t * lax.rsqrt(ms + EPS)).astype(BF16)

    def remote(src, dst, ssem, rsem, dev):
        return pltpu.make_async_remote_copy(
            src_ref=src, dst_ref=dst, send_sem=ssem, recv_sem=rsem,
            device_id=dev, device_id_type=MESH,
        )

    def right(i):
        o = lax.rem(z + NZ - i // 2, NZ)
        ref = g.at[o, lax.rem(i, 2)]
        return remote(ref, ref, agr_s.at[i], agr_r.at[i], at_z(1))

    def left(i):
        o = lax.rem(z + i // 2, NZ)
        ref = g.at[o, jnp.where(i == 6, 1, lax.rem(i, 2))]
        return remote(ref, ref, agl_s.at[i], agl_r.at[i], at_z(NZ - 1))

    def wslice(way, k):
        return lax.rem(z + NZ - 1 - k, NZ) if way == 0 else lax.rem(z + 1 + k, NZ)

    def wzr(k):
        ref = wo.at[c, lax.rem(z + NZ - k, NZ), y, x]
        return remote(ref, ref, wzr_s.at[k], wzr_r.at[k], at_z(1))

    def wzl(k):
        ref = wo.at[c, lax.rem(z + k, NZ), y, x]
        return remote(ref, ref, wzl_s.at[k], wzl_r.at[k], at_z(NZ - 1))

    def w1(way, k, d):
        ref = wo.at[c, wslice(way, k), y, x]
        n = way * 12 + k * 3 + d - 1
        dev = at_x(d) if way == 0 else at_y(d)
        return remote(ref, ref, w1_s.at[n], w1_r.at[n], dev)

    def w2(way, k, d):
        o = wslice(way, k)
        ref = wo.at[c, o, y] if way == 0 else wo.at[c, o, :, x]
        n = way * 12 + k * 3 + d - 1
        dev = at_y(d) if way == 0 else at_x(d)
        return remote(ref, ref, w2_s.at[n], w2_r.at[n], dev)

    def wcore(way, k):
        ref = wo.at[c, wslice(way, k)]
        n = way * 4 + k
        return remote(ref, ref, wc_s.at[n], wc_r.at[n], partner)

    ways = (0, 1)

    def start_w1(k, some=ways):
        for way in some:
            for d in range(1, NX):
                w1(way, k, d).start()

    def next_w2(k, some=ways):
        for way in some:
            for d in range(1, NX):
                w1(way, k, d).wait_recv()
            for d in range(1, NX):
                w2(way, k, d).start()

    def next_core(k, some=ways):
        for way in some:
            for d in range(1, NX):
                w2(way, k, d).wait_recv()
            wcore(way, k).start()

    for h in range(2):
        row = jnp.broadcast_to(wb_ref[h : h + 1, :].astype(F32), (DK, D))
        wbt[:, h * DK : (h + 1) * DK] = row.T.astype(BF16)
    cp_w3.wait()

    ri = lax.broadcasted_iota(jnp.int32, (DK, DK), 0)
    ci = lax.broadcasted_iota(jnp.int32, (DK, DK), 1)
    same = (ri // C) == (ci // C)
    strict = same & (ri > ci)
    lower = same & (ri >= ci)
    eye = jnp.where(ri == ci, 1.0, 0.0).astype(F32)

    tile8 = (ri // 8) == (ci // 8)

    def unit(v):
        return v * lax.rsqrt(jnp.sum(v * v, -1, keepdims=True) + EPS)

    def silu(v):
        return v / (1.0 + jnp.exp(-v))

    def joint(pieces):
        rows = jnp.concatenate([g[o, j] for o, j in pieces], 0)
        proj = [
            jnp.dot(rows, w3[p], preferred_element_type=F32) for p in range(3)
        ]
        pre = jnp.dot(rows, wbt[...], preferred_element_type=F32)
        qs = silu(proj[0])
        ks = silu(proj[1])
        vs = silu(proj[2])
        qh = [unit(qs[:, h * DK : (h + 1) * DK]) for h in range(2)]
        kh = [unit(ks[:, h * DK : (h + 1) * DK]) for h in range(2)]
        vh = [vs[:, h * DK : (h + 1) * DK] for h in range(2)]
        bh = [
            1.0 / (1.0 + jnp.exp(-(pre[:, h * DK : (h + 1) * DK] + bias_ref[h])))
            for h in range(2)
        ]
        def both(f, *lists):
            return [f(*args) for args in zip(*lists)]

        def stack(v):
            return [
                jnp.concatenate([v[0][a * C : (a + 1) * C], v[1][a * C : (a + 1) * C]], 0)
                for a in range(2)
            ]

        q, k, v, b = stack(qh), stack(kh), stack(vh), stack(bh)
        gram = both(lambda m: dot3(m, m, NT), k)
        low = both(lambda m, n: jnp.where(strict, m * n, 0.0), gram, b)
        near = both(lambda m: jnp.where(tile8, m, 0.0), low)
        off = both(lambda m: jnp.where(tile8, 0.0, m), low)
        rhs = both(lambda bb, kk, vv: jnp.concatenate([bb * kk, bb * vv], 1), b, k, v)
        near2 = both(dot3, near, near)
        part = both(lambda m, m2: eye - m + dot3(eye - m, m2), near, near2)
        near4 = both(dot3, near2, near2)
        masked = both(lambda m, n: jnp.where(lower, dot1(m, n, NT), 0.0), q, k)
        inv8 = both(lambda m, m4: m + dot3(m, m4), part, near4)
        step1 = both(dot3, inv8, off)
        wu = both(dot3, inv8, rhs)
        step2 = both(dot3, step1, step1)
        wu = both(lambda m, r: r - dot3(m, r), step1, wu)
        step4 = both(dot3, step2, step2)
        wu = both(lambda m, r: r + dot3(m, r), step2, wu)
        wu = both(lambda m, r: r + dot3(m, r), step4, wu)
        mwu = both(dot1, masked, wu)
        pairs = []
        for a in range(2):
            for h in range(2):
                hp = slice(h * C, (h + 1) * C)
                pairs.append(dot3(wu[a][hp], k[a][hp], TN))
        for a, (o, j) in enumerate(pieces):
            blk = 2 * o + j
            for h in range(2):
                hp = slice(h * C, (h + 1) * C)
                pair = pairs[2 * a + h]
                qe[h, blk] = q[a][hp] - mwu[a][hp, :DK]
                mu[h, blk] = mwu[a][hp, DK:]
                db[h, blk, :DK] = -pair[:DK]
                db[h, blk, DK:] = pair[DK:]

    last = lax.rem(z + NZ // 2, NZ)
    zero = jnp.zeros((2 * DK, DK), F32)

    def close_chunk(o):
        for h in range(2):
            d0 = db[h, 2 * o]
            q = qe[h, 2 * o + 1]
            both = dot1(q, d0, NT)
            qe[h, 2 * o + 1] = q + both[:, :DK]
            mu[h, 2 * o + 1] = mu[h, 2 * o + 1] + both[:, DK:]
            ct[h, o] = compose(d0, db[h, 2 * o + 1])

    def run_chain(o, carry):
        nxt = []
        for h in range(2):
            here = ct[h, o]
            ct[h, o] = carry[h]
            nxt.append(compose(carry[h], here))
        return tuple(nxt)

    def work(oa, ja, ob, jb, closing):
        joint([(oa, ja), (ob, jb)])

        def close(n, carry):
            close_chunk(jnp.where(n == 0, oa, ob))
            return carry

        lax.fori_loop(0, closing, close, 0)

    work(z, 0, z, 1, 1)

    for cp in cp_wo:
        cp.wait()
    pl.semaphore_wait(barrier, len(peers))
    for i in range(2):
        right(jnp.int32(i)).start()
        left(jnp.int32(i)).start()
        if i == 0:
            wzr(0).start()
            wzl(0).start()

    def step(t, carry):
        i = t - 1
        mid = t <= 6
        even = lax.rem(t, 2) == 0

        @pl.when(t == 7)
        def _():
            for n, (lo, hi) in enumerate(((0, last), (last + 1, NZ))):
                got = lax.fori_loop(lo, hi, run_chain, (zero, zero))
                for h in range(2):
                    ends[n, h] = got[h]

        def receive():
            @pl.when(even)
            def _():
                k = t // 2 - 1
                wzr(k).wait_recv()
                wzr(k + 1).start()
                wzl(k).wait_recv()

                @pl.when(k <= 1)
                def _():
                    wzl(k + 1).start()

            right(i).wait_recv()

            @pl.when(i <= 4)
            def _():
                right(i + 2).start()

            left(i).wait_recv()

            @pl.when(i <= 3)
            def _():
                left(i + 2).start()

            @pl.when(i == 5)
            def _():
                left(i + 1).start()

            @pl.when(even)
            def _():
                k = t // 2 - 1
                start_w1(k)

                @pl.when(k >= 1)
                def _():
                    next_core(k - 1)

            @pl.when(jnp.logical_and(t >= 3, jnp.logical_not(even)))
            def _():
                next_w2((t - 3) // 2)

            @pl.when(t == 7)
            def _():
                wzr(3).wait_recv()
                start_w1(3, (0,))

        receive()
        hop = (i + 2) // 2
        ja = jnp.where(mid, lax.rem(i, 2), 0)
        jb = jnp.where(mid, lax.rem(i, 2), 1)
        oa = lax.rem(z + NZ - hop, NZ)
        ob = lax.rem(z + hop, NZ)
        work(oa, ja, ob, jb, jnp.where(mid, jnp.where(even, 2, 0), 1))
        return carry

    lax.fori_loop(1, 8, step, 0)

    next_w2(3, (0,))
    for h in range(2):
        pre = ends[0, h]
        upto = compose(pre, ct[h, last])
        ct[h, last] = pre
        tot[h] = compose(upto, ends[1, h])
        ends[0, h] = upto

    def core_swap():
        return remote(tot.at[1 - c], lv.at[c], sc_s.at[0], sc_r.at[0], partner)

    core_swap().start()
    lv[c] = tot[c]

    def fold_queries(first, final):
        def one(o, carry):
            after = jnp.broadcast_to((o > last).astype(jnp.int32), (2 * DK, DK)) > 0
            for h in range(2):
                m = compose(jnp.where(after, ends[0, h], 0.0), ct[h, o])
                q = jnp.concatenate([qe[h, 2 * o], qe[h, 2 * o + 1]], 0)
                both = dot1(q, m, NT)
                new = q + both[:, :DK]
                qe[h, 2 * o] = new[:C]
                qe[h, 2 * o + 1] = new[C:]
                mu[h, 2 * o] = mu[h, 2 * o] + both[:C, DK:]
                mu[h, 2 * o + 1] = mu[h, 2 * o + 1] + both[C:, DK:]
            return carry

        lax.fori_loop(first, final, one, 0)

    core_swap().wait_recv()

    group = compose(lv[0], lv[1])
    before = jnp.zeros((2 * DK, DK), F32)
    xp = jnp.where(lax.rem(x, 2) == 0, 1, NX - 1)
    yp = jnp.where(lax.rem(y, 2) == 0, 1, NY - 1)
    xq = lax.rem(2 * NX - 1 - 2 * x, NX)
    yq = lax.rem(2 * NY - 1 - 2 * y, NY)
    levels = [
        (at_x(xp), lax.rem(x, 2) == 0),
        (at_x(xq), x < 2),
        (at_y(yp), lax.rem(y, 2) == 0),
        (at_y(yq), y < 2),
    ]
    sends = []
    for n, (dev, is_low) in enumerate(levels[:3]):
        xs[n] = group.astype(BF16)
        cp = remote(xs.at[n], xr.at[n], sc_s.at[n + 1], sc_r.at[n + 1], dev)
        cp.start()
        sends.append(cp)
        fold_queries(2 * n, 2 * n + 2)
        cp.wait_recv()
        other = xr[n].astype(F32)
        low = jnp.broadcast_to(is_low.astype(jnp.int32), (2 * DK, DK)) > 0
        group = compose(jnp.where(low, group, other), jnp.where(low, other, group))
        before = jnp.where(low, before, compose(other, before))
        if n == 0:
            next_core(2)
        if n == 1:
            next_core(3, (0,))

    ys[...] = group[DK:].astype(BF16)
    far, _ = levels[3]
    for q in range(NC):
        dev = (far[0] - c + q, z)
        cp = remote(ys, yr.at[c], sc_s.at[4 + q], sc_r.at[4 + c], dev)
        cp.start()
        sends.append(cp)

    def got_y(h):
        return remote(ys, yr.at[h], sc_s.at[4 + h], sc_r.at[4 + h], partner)

    before1 = compose(before, lv[0])
    zero_core = jnp.broadcast_to(c, (2 * DK, DK)) == 0
    es[...] = jnp.where(zero_core, before1, before)
    give = remote(es, eb.at[c], sc_s.at[6], sc_r.at[6], partner)
    give.start()
    eb[c] = jnp.where(zero_core, before, before1)
    fold_queries(6, 8)
    give.wait_recv()
    high = jnp.broadcast_to((y >= 2).astype(jnp.int32), (DK, DK)) > 0
    sin = []
    for h in range(2):
        got_y(h).wait_recv()
        base = jnp.where(high, yr[h].astype(F32), 0.0)
        sin.append(base + dot3(base, eb[h, :DK]) + eb[h, DK:])
    for h in range(2):
        sf[h] = sin[h]

    def a2a(d, o):
        return remote(osend.at[o], fbuf.at[z], a2_s.at[d - 1], a2_r.at[d - 1], (s, o))

    def emit(i, carry):
        d = jnp.where(lax.rem(i, 2) == 1, 4 - (i + 1) // 2, 4 + i // 2)
        o = lax.rem(z + d, NZ)
        cols = []
        for h in range(2):
            q = jnp.concatenate([qe[h, 2 * o], qe[h, 2 * o + 1]], 0)
            m = jnp.concatenate([mu[h, 2 * o], mu[h, 2 * o + 1]], 0)
            full = m + dot1(q, sf[h], NT)
            ms = jnp.mean(full * full, -1, keepdims=True)
            cols.append((full * lax.rsqrt(ms + EPS)).astype(BF16))
        rows = jnp.concatenate(cols, 1)

        @pl.when(i < 7)
        def _():
            osend[o] = rows
            a2a(d, o).start()

        @pl.when(i == 7)
        def _():
            fbuf[z] = rows

        return carry

    lax.fori_loop(0, NZ, emit, 0)

    for k in range(4):
        wcore(0, k).wait_recv()
        if k < 3:
            wcore(1, k).wait_recv()

    def finish(i, carry):
        n = i - 1
        d = jnp.where(lax.rem(n, 2) == 1, 4 - (n + 1) // 2, 4 + n // 2)
        d = jnp.where(i == 0, 0, d)
        src = lax.rem(z + NZ - d, NZ)

        @pl.when(i >= 1)
        def _():
            remote(
                osend.at[src], fbuf.at[src], a2_s.at[d - 1], a2_r.at[d - 1], (s, src)
            ).wait_recv()

        rows = fbuf[src]
        for half in range(2):
            w = wo[half, src].reshape(2 * DK, 1024)
            term = jnp.dot(rows, w, preferred_element_type=F32)
            cols = slice(half * 1024, (half + 1) * 1024)

            @pl.when(i == 0)
            def _():
                acc[:, cols] = term

            @pl.when(i >= 1)
            def _():
                acc[:, cols] = acc[:, cols] + term

        return carry

    lax.fori_loop(0, NZ, finish, 0)
    out_ref[...] = acc[...].astype(BF16)

    for i in range(7):
        right(jnp.int32(i)).wait_send()
        left(jnp.int32(i)).wait_send()
    for d in range(1, NZ):
        a2a(d, lax.rem(z + d, NZ)).wait_send()
    for k in range(4):
        wzr(k).wait_send()
        for way in ways[: 2 if k < 3 else 1]:
            wcore(way, k).wait_send()
            for d in range(1, NX):
                w1(way, k, d).wait_send()
                w2(way, k, d).wait_send()
        if k < 3:
            wzl(k).wait_send()
    core_swap().wait_send()
    for cp in sends:
        cp.wait_send()
    give.wait_send()


def body(tokens, w_qkv, w_beta, beta_bias, w_out):
    w3 = jnp.transpose(w_qkv, (1, 0, 2))
    wb = jnp.transpose(w_beta, (1, 0))
    wo = w_out.reshape(NY, NX, 16, D)
    vmem = pl.BlockSpec(memory_space=pltpu.VMEM)
    hbm = pl.BlockSpec(memory_space=pl.ANY)
    smem = pl.BlockSpec(memory_space=pltpu.SMEM)
    dma = pltpu.SemaphoreType.DMA
    return pl.pallas_call(
        kernel,
        out_shape=jax.ShapeDtypeStruct((2 * C, D), BF16),
        in_specs=[vmem, hbm, vmem, smem, hbm],
        out_specs=vmem,
        scratch_shapes=[
            pltpu.VMEM((NZ, 2, C, D), BF16),
            pltpu.VMEM((3, D, 2 * DK), BF16),
            pltpu.VMEM((D, 2 * DK), BF16),
            pltpu.VMEM((2, NZ, NY, NX, 16, 1024), BF16),
            pltpu.VMEM((2, 16, C, DK), F32),
            pltpu.VMEM((2, 16, C, DK), F32),
            pltpu.VMEM((2, 16, 2 * DK, DK), F32),
            pltpu.VMEM((2, NZ, 2 * DK, DK), F32),
            pltpu.VMEM((2, 2, 2 * DK, DK), F32),
            pltpu.VMEM((2, 2 * DK, DK), F32),
            pltpu.VMEM((2, 2 * DK, DK), F32),
            pltpu.VMEM((3, 2 * DK, DK), BF16),
            pltpu.VMEM((3, 2 * DK, DK), BF16),
            pltpu.VMEM((DK, DK), BF16),
            pltpu.VMEM((2, DK, DK), BF16),
            pltpu.VMEM((2, 2 * DK, DK), F32),
            pltpu.VMEM((2 * DK, DK), F32),
            pltpu.VMEM((2, DK, DK), F32),
            pltpu.VMEM((NZ, 2 * C, 2 * DK), BF16),
            pltpu.VMEM((NZ, 2 * C, 2 * DK), BF16),
            pltpu.VMEM((2 * C, D), F32),
            dma((3,)),
            dma((7,)),
            dma((7,)),
            dma((7,)),
            dma((7,)),
            dma((4,)),
            dma((4,)),
            dma((3,)),
            dma((3,)),
            dma((21,)),
            dma((21,)),
            dma((21,)),
            dma((21,)),
            dma((7,)),
            dma((7,)),
            dma((7,)),
            dma((7,)),
            dma((7,)),
            dma((7,)),
        ],
        compiler_params=pltpu.CompilerParams(
            collective_id=0, has_side_effects=True, vmem_limit_bytes=60 * 1024 * 1024
        ),
        name="delta_layer",
    )(tokens, w3, wb, beta_bias, wo)


def solution(mesh):
    return jax.shard_map(
        body,
        mesh=mesh,
        in_specs=(
            P(("seq", "head"), None),
            P(None, None, "head"),
            P(None, "head"),
            P("head"),
            P("head", None),
        ),
        out_specs=P(("seq", "head"), None),
        check_vma=False,
    )
```

```python
import jax
import jax.numpy as jnp
from jax import lax
from jax.experimental import pallas as pl
from jax.experimental.pallas import tpu as pltpu
from jax.sharding import PartitionSpec as P

F32 = jnp.float32
BF16 = jnp.bfloat16
MESH = pl.DeviceIdType.MESH
EPS = 1e-6
NZ = 8
NX = 4
NY = 4
NC = 2
C = 64
DK = 128
D = 2048

NN = (((1,), (0,)), ((), ()))
NT = (((1,), (1,)), ((), ()))
TN = (((0,), (0,)), ((), ()))


def halves(a):
    hi = a.astype(BF16)
    lo = (a - hi.astype(F32)).astype(BF16)
    return hi, lo


def dot3(a, b, dims=NN):
    ca = dims[0][0][0]
    cb = dims[0][1][0]
    ah, al = halves(a)
    bh, bl = halves(b)
    return lax.dot_general(
        jnp.concatenate([ah, al, ah], ca),
        jnp.concatenate([bh, bh, bl], cb),
        dims,
        preferred_element_type=F32,
    )


def dot1(a, b, dims=NN):
    return lax.dot_general(
        a.astype(BF16), b.astype(BF16), dims, preferred_element_type=F32
    )


def compose(first, second):
    return first + dot3(first, second[:DK]) + second


def kernel(
    tok_ref,
    w3_hbm,
    wb_ref,
    bias_ref,
    wo_hbm,
    out_ref,
    g,
    w3,
    wbt,
    wo,
    qe,
    mu,
    db,
    ct,
    ends,
    tot,
    lv,
    xs,
    xr,
    xg,
    ys,
    yr,
    eb,
    es,
    sf,
    osend,
    fbuf,
    acc,
    lsem,
    agr_s,
    agr_r,
    agl_s,
    agl_r,
    wzr_s,
    wzr_r,
    wzl_s,
    wzl_r,
    w1_s,
    w1_r,
    w2_s,
    w2_r,
    wc_s,
    wc_r,
    sc_s,
    sc_r,
    a2_s,
    a2_r,
):
    s = lax.axis_index("seq")
    z = lax.axis_index("head")
    c = lax.rem(s, NC)
    x = lax.rem(s // NC, NX)
    y = s // (NC * NX)

    def at_z(d):
        return (s, lax.rem(z + d, NZ))

    def at_x(d):
        return ((y * NX + lax.rem(x + d, NX)) * NC + c, z)

    def at_y(d):
        return ((lax.rem(y + d, NY) * NX + x) * NC + c, z)

    partner = ((y * NX + x) * NC + (1 - c), z)

    peers = [at_z(1), at_z(NZ - 1)]
    peers += [at_x(d) for d in range(1, NX)]
    peers += [at_y(d) for d in range(1, NY)]
    peers += [partner]
    barrier = pltpu.get_barrier_semaphore()
    for p in peers:
        pl.semaphore_signal(barrier, inc=1, device_id=p, device_id_type=MESH)

    cp_w3 = pltpu.make_async_copy(w3_hbm, w3, lsem.at[0])
    cp_w3.start()
    cp_wo = [
        pltpu.make_async_copy(
            wo_hbm.at[:, :, :, pl.ds(q * 1024, 1024)], wo.at[q, z], lsem.at[1 + q]
        )
        for q in range(NC)
    ]
    for cp in cp_wo:
        cp.start()

    for j in range(2):
        t = tok_ref[j * C : (j + 1) * C, :].astype(F32)
        ms = jnp.mean(t * t, -1, keepdims=True)
        g[z, j] = (t * lax.rsqrt(ms + EPS)).astype(BF16)

    def remote(src, dst, ssem, rsem, dev):
        return pltpu.make_async_remote_copy(
            src_ref=src, dst_ref=dst, send_sem=ssem, recv_sem=rsem,
            device_id=dev, device_id_type=MESH,
        )

    def right(i):
        o = lax.rem(z + NZ - i // 2, NZ)
        ref = g.at[o, lax.rem(i, 2)]
        return remote(ref, ref, agr_s.at[i], agr_r.at[i], at_z(1))

    def left(i):
        o = lax.rem(z + i // 2, NZ)
        ref = g.at[o, jnp.where(i == 6, 1, lax.rem(i, 2))]
        return remote(ref, ref, agl_s.at[i], agl_r.at[i], at_z(NZ - 1))

    def wslice(way, k):
        return lax.rem(z + NZ - 1 - k, NZ) if way == 0 else lax.rem(z + 1 + k, NZ)

    def wzr(k):
        ref = wo.at[c, lax.rem(z + NZ - k, NZ), y, x]
        return remote(ref, ref, wzr_s.at[k], wzr_r.at[k], at_z(1))

    def wzl(k):
        ref = wo.at[c, lax.rem(z + k, NZ), y, x]
        return remote(ref, ref, wzl_s.at[k], wzl_r.at[k], at_z(NZ - 1))

    def w1(way, k, d):
        ref = wo.at[c, wslice(way, k), y, x]
        n = way * 12 + k * 3 + d - 1
        dev = at_x(d) if way == 0 else at_y(d)
        return remote(ref, ref, w1_s.at[n], w1_r.at[n], dev)

    def w2(way, k, d):
        o = wslice(way, k)
        ref = wo.at[c, o, y] if way == 0 else wo.at[c, o, :, x]
        n = way * 12 + k * 3 + d - 1
        dev = at_y(d) if way == 0 else at_x(d)
        return remote(ref, ref, w2_s.at[n], w2_r.at[n], dev)

    def wcore(way, k):
        ref = wo.at[c, wslice(way, k)]
        n = way * 4 + k
        return remote(ref, ref, wc_s.at[n], wc_r.at[n], partner)

    ways = (0, 1)

    def start_w1(k, some=ways):
        for way in some:
            for d in range(1, NX):
                w1(way, k, d).start()

    def next_w2(k, some=ways):
        for way in some:
            for d in range(1, NX):
                w1(way, k, d).wait_recv()
            for d in range(1, NX):
                w2(way, k, d).start()

    def next_core(k, some=ways):
        for way in some:
            for d in range(1, NX):
                w2(way, k, d).wait_recv()
            wcore(way, k).start()

    wbt[...] = jnp.concatenate(
        [wb_ref[...].astype(F32), jnp.zeros((DK - 2, D), F32)], 0
    ).T.astype(BF16)

    for cp in cp_wo:
        cp.wait()
    pl.semaphore_wait(barrier, len(peers))
    wzr(0).start()
    wzl(0).start()
    for i in range(2):
        right(jnp.int32(i)).start()
        left(jnp.int32(i)).start()
    cp_w3.wait()

    ri = lax.broadcasted_iota(jnp.int32, (DK, DK), 0)
    ci = lax.broadcasted_iota(jnp.int32, (DK, DK), 1)
    same = (ri // C) == (ci // C)
    strict = same & (ri > ci)
    lower = same & (ri >= ci)
    eye = jnp.where(ri == ci, 1.0, 0.0).astype(F32)

    tile8 = (ri // 8) == (ci // 8)

    def unit(v):
        return v * lax.rsqrt(jnp.sum(v * v, -1, keepdims=True) + EPS)

    def silu(v):
        return v / (1.0 + jnp.exp(-v))

    def joint(pieces):
        rows = jnp.concatenate([g[o, j] for o, j in pieces], 0)
        proj = [
            jnp.dot(rows, w3[p], preferred_element_type=F32) for p in range(3)
        ]
        pre = jnp.dot(rows, wbt[...], preferred_element_type=F32)
        qs = silu(proj[0])
        ks = silu(proj[1])
        vs = silu(proj[2])
        qh = [unit(qs[:, h * DK : (h + 1) * DK]) for h in range(2)]
        kh = [unit(ks[:, h * DK : (h + 1) * DK]) for h in range(2)]
        vh = [vs[:, h * DK : (h + 1) * DK] for h in range(2)]
        bh = [
            1.0 / (1.0 + jnp.exp(-(jnp.broadcast_to(pre[:, h : h + 1], (DK, DK)) + bias_ref[h])))
            for h in range(2)
        ]
        def both(f, *lists):
            return [f(*args) for args in zip(*lists)]

        def stack(v):
            return [
                jnp.concatenate([v[0][a * C : (a + 1) * C], v[1][a * C : (a + 1) * C]], 0)
                for a in range(2)
            ]

        q, k, v, b = stack(qh), stack(kh), stack(vh), stack(bh)
        gram = both(lambda m: dot3(m, m, NT), k)
        low = both(lambda m, n: jnp.where(strict, m * n, 0.0), gram, b)
        near = both(lambda m: jnp.where(tile8, m, 0.0), low)
        off = both(lambda m: jnp.where(tile8, 0.0, m), low)
        rhs = both(lambda bb, kk, vv: jnp.concatenate([bb * kk, bb * vv], 1), b, k, v)
        near2 = both(dot3, near, near)
        part = both(lambda m, m2: eye - m + dot3(eye - m, m2), near, near2)
        near4 = both(dot3, near2, near2)
        masked = both(lambda m, n: jnp.where(lower, dot1(m, n, NT), 0.0), q, k)
        inv8 = both(lambda m, m4: m + dot3(m, m4), part, near4)
        step1 = both(dot3, inv8, off)
        wu = both(dot3, inv8, rhs)
        step2 = both(dot3, step1, step1)
        wu = both(lambda m, r: r - dot3(m, r), step1, wu)
        step4 = both(dot3, step2, step2)
        wu = both(lambda m, r: r + dot3(m, r), step2, wu)
        wu = both(lambda m, r: r + dot3(m, r), step4, wu)
        mwu = both(dot1, masked, wu)
        pairs = []
        for a in range(2):
            for h in range(2):
                hp = slice(h * C, (h + 1) * C)
                pairs.append(dot3(wu[a][hp], k[a][hp], TN))
        for a, (o, j) in enumerate(pieces):
            blk = 2 * o + j
            for h in range(2):
                hp = slice(h * C, (h + 1) * C)
                pair = pairs[2 * a + h]
                qe[h, blk] = q[a][hp] - mwu[a][hp, :DK]
                mu[h, blk] = mwu[a][hp, DK:]
                db[h, blk, :DK] = -pair[:DK]
                db[h, blk, DK:] = pair[DK:]

    last = lax.rem(z + NZ // 2, NZ)
    zero = jnp.zeros((2 * DK, DK), F32)

    def fold_second(o, h):
        q = qe[h, 2 * o + 1]
        both = dot1(q, db[h, 2 * o], NT)
        qe[h, 2 * o + 1] = q + both[:, :DK]
        mu[h, 2 * o + 1] = mu[h, 2 * o + 1] + both[:, DK:]

    def close_chunk(o):
        for h in range(2):
            fold_second(o, h)
            ct[h, o] = compose(db[h, 2 * o], db[h, 2 * o + 1])

    def run_chain(o, carry):
        nxt = []
        for h in range(2):
            here = ct[h, o]
            ct[h, o] = carry[h]
            nxt.append(compose(carry[h], here))
        return tuple(nxt)

    def work(oa, ja, ob, jb, closing):
        joint([(oa, ja), (ob, jb)])

        def close(n, carry):
            close_chunk(jnp.where(n == 0, oa, ob))
            return carry

        lax.fori_loop(0, closing, close, 0)

    work(z, 0, z, 1, 1)

    def step(t, carry):
        i = t - 1
        mid = t <= 6
        even = lax.rem(t, 2) == 0

        @pl.when(t == 7)
        def _():
            wzr(3).wait_recv()
            start_w1(3, (0,))
            for n, (lo, hi) in enumerate(((0, last), (last + 1, NZ))):
                got = lax.fori_loop(lo, hi, run_chain, (zero, zero))
                for h in range(2):
                    ends[n, h] = got[h]

        early = jnp.logical_and(jnp.logical_not(even), mid)

        @pl.when(early)
        def _():
            k = i // 2
            wzr(k).wait_recv()
            wzr(k + 1).start()
            wzl(k).wait_recv()

            @pl.when(k <= 1)
            def _():
                wzl(k + 1).start()

        right(i).wait_recv()

        @pl.when(i <= 4)
        def _():
            right(i + 2).start()

        left(i).wait_recv()

        @pl.when(i <= 3)
        def _():
            left(i + 2).start()

        @pl.when(i == 5)
        def _():
            left(i + 1).start()

        @pl.when(early)
        def _():
            start_w1(i // 2)

        @pl.when(even)
        def _():
            next_w2(t // 2 - 1)

            @pl.when(t >= 4)
            def _():
                next_core(t // 2 - 2)

        @pl.when(t == 7)
        def _():
            next_w2(3, (0,))

        hop = (i + 2) // 2
        ja = jnp.where(mid, lax.rem(i, 2), 0)
        jb = jnp.where(mid, lax.rem(i, 2), 1)
        oa = lax.rem(z + NZ - hop, NZ)
        ob = lax.rem(z + hop, NZ)
        work(oa, ja, ob, jb, jnp.where(jnp.logical_and(mid, even), 2, 0))
        return carry

    lax.fori_loop(1, 8, step, 0)

    head = [compose(ends[0, h], db[h, 2 * last]) for h in range(2)]
    rest = [compose(db[h, 2 * last + 1], ends[1, h]) for h in range(2)]
    for h in range(2):
        tot[h] = compose(head[h], rest[h])

    def core_swap():
        return remote(tot.at[1 - c], lv.at[c], sc_s.at[0], sc_r.at[0], partner)

    core_swap().start()
    lv[c] = tot[c]

    def fold_queries(first, final):
        def one(o, carry):
            after = jnp.broadcast_to((o > last).astype(jnp.int32), (2 * DK, DK)) > 0
            for h in range(2):
                m = compose(jnp.where(after, ends[0, h], 0.0), ct[h, o])
                q = jnp.concatenate([qe[h, 2 * o], qe[h, 2 * o + 1]], 0)
                both = dot1(q, m, NT)
                new = q + both[:, :DK]
                qe[h, 2 * o] = new[:C]
                qe[h, 2 * o + 1] = new[C:]
                mu[h, 2 * o] = mu[h, 2 * o] + both[:C, DK:]
                mu[h, 2 * o + 1] = mu[h, 2 * o + 1] + both[C:, DK:]
            return carry

        lax.fori_loop(first, final, one, 0)

    for h in range(2):
        ct[h, last] = ends[0, h]
        ends[0, h] = compose(head[h], db[h, 2 * last + 1])
        fold_second(last, h)
    core_swap().wait_recv()

    group = compose(lv[0], lv[1])
    sends = []
    xs[0] = group.astype(BF16)
    for d in range(1, NX):
        cp = remote(xs.at[0], xg.at[x], sc_s.at[d], sc_r.at[d], at_x(d))
        cp.start()
        sends.append(cp)
    xg[x] = group.astype(BF16)
    fold_queries(0, 4)
    for d in range(1, NX):
        sends[d - 1].wait_recv()
    part = [xg[n].astype(F32) for n in range(NX)]
    p01 = compose(part[0], part[1])
    p23 = compose(part[2], part[3])
    p012 = compose(p01, part[2])
    group = compose(p01, p23)
    xv = jnp.broadcast_to(x, (2 * DK, DK))
    before = jnp.where(xv == 1, part[0], 0.0)
    before = jnp.where(xv == 2, p01, before)
    before = jnp.where(xv == 3, p012, before)

    yp = jnp.where(lax.rem(y, 2) == 0, 1, NY - 1)
    yq = lax.rem(2 * NY - 1 - 2 * y, NY)
    xs[1] = group.astype(BF16)
    cp = remote(xs.at[1], xr, sc_s.at[7], sc_r.at[7], at_y(yp))
    cp.start()
    sends.append(cp)
    next_core(2)
    fold_queries(4, 6)
    cp.wait_recv()
    other = xr[...].astype(F32)
    low = jnp.broadcast_to(lax.rem(y, 2), (2 * DK, DK)) == 0
    group = compose(jnp.where(low, group, other), jnp.where(low, other, group))
    before = jnp.where(low, before, compose(other, before))

    ys[...] = group[DK:].astype(BF16)
    far = at_y(yq)
    for q in range(NC):
        dev = (far[0] - c + q, z)
        cp = remote(ys, yr.at[c], sc_s.at[4 + q], sc_r.at[4 + c], dev)
        cp.start()
        sends.append(cp)

    def got_y(h):
        return remote(ys, yr.at[h], sc_s.at[4 + h], sc_r.at[4 + h], partner)

    before1 = compose(before, lv[0])
    zero_core = jnp.broadcast_to(c, (2 * DK, DK)) == 0
    es[...] = jnp.where(zero_core, before1, before)
    give = remote(es, eb.at[c], sc_s.at[6], sc_r.at[6], partner)
    give.start()
    eb[c] = jnp.where(zero_core, before, before1)
    next_core(3, (0,))
    fold_queries(6, 8)
    give.wait_recv()
    high = jnp.broadcast_to((y >= 2).astype(jnp.int32), (DK, DK)) > 0
    sin = []
    for h in range(2):
        got_y(h).wait_recv()
        base = jnp.where(high, yr[h].astype(F32), 0.0)
        sin.append(base + dot3(base, eb[h, :DK]) + eb[h, DK:])
    for h in range(2):
        sf[h] = sin[h]

    def a2a(d, o):
        return remote(osend.at[o], fbuf.at[z], a2_s.at[d - 1], a2_r.at[d - 1], (s, o))

    def emit(i, carry):
        d = jnp.where(lax.rem(i, 2) == 1, 4 - (i + 1) // 2, 4 + i // 2)
        o = lax.rem(z + d, NZ)
        cols = []
        for h in range(2):
            q = jnp.concatenate([qe[h, 2 * o], qe[h, 2 * o + 1]], 0)
            m = jnp.concatenate([mu[h, 2 * o], mu[h, 2 * o + 1]], 0)
            full = m + dot1(q, sf[h], NT)
            ms = jnp.mean(full * full, -1, keepdims=True)
            cols.append((full * lax.rsqrt(ms + EPS)).astype(BF16))
        rows = jnp.concatenate(cols, 1)

        @pl.when(i < 7)
        def _():
            osend[o] = rows
            a2a(d, o).start()

        @pl.when(i == 7)
        def _():
            fbuf[z] = rows

        return carry

    lax.fori_loop(0, NZ, emit, 0)

    for k in range(4):
        wcore(0, k).wait_recv()
        if k < 3:
            wcore(1, k).wait_recv()

    def finish(i, carry):
        n = i - 1
        d = jnp.where(lax.rem(n, 2) == 1, 4 - (n + 1) // 2, 4 + n // 2)
        d = jnp.where(i == 0, 0, d)
        src = lax.rem(z + NZ - d, NZ)

        @pl.when(i >= 1)
        def _():
            remote(
                osend.at[src], fbuf.at[src], a2_s.at[d - 1], a2_r.at[d - 1], (s, src)
            ).wait_recv()

        rows = fbuf[src]
        for half in range(2):
            w = wo[half, src].reshape(2 * DK, 1024)
            term = jnp.dot(rows, w, preferred_element_type=F32)
            cols = slice(half * 1024, (half + 1) * 1024)

            @pl.when(i == 0)
            def _():
                acc[:, cols] = term

            @pl.when(i >= 1)
            def _():
                acc[:, cols] = acc[:, cols] + term

        return carry

    lax.fori_loop(0, NZ, finish, 0)
    out_ref[...] = acc[...].astype(BF16)

    for i in range(7):
        right(jnp.int32(i)).wait_send()
        left(jnp.int32(i)).wait_send()
    for d in range(1, NZ):
        a2a(d, lax.rem(z + d, NZ)).wait_send()
    for k in range(4):
        wzr(k).wait_send()
        for way in ways[: 2 if k < 3 else 1]:
            wcore(way, k).wait_send()
            for d in range(1, NX):
                w1(way, k, d).wait_send()
                w2(way, k, d).wait_send()
        if k < 3:
            wzl(k).wait_send()
    core_swap().wait_send()
    for cp in sends:
        cp.wait_send()
    give.wait_send()


def body(tokens, w_qkv, w_beta, beta_bias, w_out):
    w3 = jnp.transpose(w_qkv, (1, 0, 2))
    wb = jnp.transpose(w_beta, (1, 0))
    wo = w_out.reshape(NY, NX, 16, D)
    vmem = pl.BlockSpec(memory_space=pltpu.VMEM)
    hbm = pl.BlockSpec(memory_space=pl.ANY)
    smem = pl.BlockSpec(memory_space=pltpu.SMEM)
    dma = pltpu.SemaphoreType.DMA
    return pl.pallas_call(
        kernel,
        out_shape=jax.ShapeDtypeStruct((2 * C, D), BF16),
        in_specs=[vmem, hbm, vmem, smem, hbm],
        out_specs=vmem,
        scratch_shapes=[
            pltpu.VMEM((NZ, 2, C, D), BF16),
            pltpu.VMEM((3, D, 2 * DK), BF16),
            pltpu.VMEM((D, DK), BF16),
            pltpu.VMEM((2, NZ, NY, NX, 16, 1024), BF16),
            pltpu.VMEM((2, 16, C, DK), F32),
            pltpu.VMEM((2, 16, C, DK), F32),
            pltpu.VMEM((2, 16, 2 * DK, DK), F32),
            pltpu.VMEM((2, NZ, 2 * DK, DK), F32),
            pltpu.VMEM((2, 2, 2 * DK, DK), F32),
            pltpu.VMEM((2, 2 * DK, DK), F32),
            pltpu.VMEM((2, 2 * DK, DK), F32),
            pltpu.VMEM((2, 2 * DK, DK), BF16),
            pltpu.VMEM((2 * DK, DK), BF16),
            pltpu.VMEM((NX, 2 * DK, DK), BF16),
            pltpu.VMEM((DK, DK), BF16),
            pltpu.VMEM((2, DK, DK), BF16),
            pltpu.VMEM((2, 2 * DK, DK), F32),
            pltpu.VMEM((2 * DK, DK), F32),
            pltpu.VMEM((2, DK, DK), F32),
            pltpu.VMEM((NZ, 2 * C, 2 * DK), BF16),
            pltpu.VMEM((NZ, 2 * C, 2 * DK), BF16),
            pltpu.VMEM((2 * C, D), F32),
            dma((3,)),
            dma((7,)),
            dma((7,)),
            dma((7,)),
            dma((7,)),
            dma((4,)),
            dma((4,)),
            dma((3,)),
            dma((3,)),
            dma((21,)),
            dma((21,)),
            dma((21,)),
            dma((21,)),
            dma((7,)),
            dma((7,)),
            dma((8,)),
            dma((8,)),
            dma((7,)),
            dma((7,)),
        ],
        compiler_params=pltpu.CompilerParams(
            collective_id=0, has_side_effects=True, vmem_limit_bytes=60 * 1024 * 1024
        ),
        name="delta_layer",
    )(tokens, w3, wb, beta_bias, wo)


def solution(mesh):
    return jax.shard_map(
        body,
        mesh=mesh,
        in_specs=(
            P(("seq", "head"), None),
            P(None, None, "head"),
            P(None, "head"),
            P("head"),
            P("head", None),
        ),
        out_specs=P(("seq", "head"), None),
        check_vma=False,
    )
```

```python
import jax
import jax.numpy as jnp
from jax import lax
from jax.experimental import pallas as pl
from jax.experimental.pallas import tpu as pltpu
from jax.sharding import PartitionSpec as P

F32 = jnp.float32
BF16 = jnp.bfloat16
MESH = pl.DeviceIdType.MESH
EPS = 1e-6
NZ = 8
NX = 4
NY = 4
NC = 2
C = 64
DK = 128
D = 2048

NN = (((1,), (0,)), ((), ()))
NT = (((1,), (1,)), ((), ()))
TN = (((0,), (0,)), ((), ()))


def halves(a):
    hi = a.astype(BF16)
    lo = (a - hi.astype(F32)).astype(BF16)
    return hi, lo


def dot3(a, b, dims=NN):
    ca = dims[0][0][0]
    cb = dims[0][1][0]
    ah, al = halves(a)
    bh, bl = halves(b)
    return lax.dot_general(
        jnp.concatenate([ah, al, ah], ca),
        jnp.concatenate([bh, bh, bl], cb),
        dims,
        preferred_element_type=F32,
    )


def dot1(a, b, dims=NN):
    return lax.dot_general(
        a.astype(BF16), b.astype(BF16), dims, preferred_element_type=F32
    )


def compose(first, second):
    return first + dot3(first, second[:DK]) + second


def kernel(
    tok_ref,
    w3_hbm,
    wb_ref,
    bias_ref,
    wo_hbm,
    out_ref,
    g,
    w3,
    wbt,
    wo,
    qe,
    mu,
    db,
    ct,
    ends,
    tot,
    lv,
    xs,
    xr,
    xg,
    ys,
    yr,
    eb,
    es,
    sf,
    osend,
    fbuf,
    acc,
    hello,
    lsem,
    agr_s,
    agr_r,
    agl_s,
    agl_r,
    wzr_s,
    wzr_r,
    wzl_s,
    wzl_r,
    w1_s,
    w1_r,
    w2_s,
    w2_r,
    wc_s,
    wc_r,
    sc_s,
    sc_r,
    a2_s,
    a2_r,
):
    s = lax.axis_index("seq")
    z = lax.axis_index("head")
    c = lax.rem(s, NC)
    x = lax.rem(s // NC, NX)
    y = s // (NC * NX)

    def at_z(d):
        return (s, lax.rem(z + d, NZ))

    def at_x(d):
        return ((y * NX + lax.rem(x + d, NX)) * NC + c, z)

    def at_y(d):
        return ((lax.rem(y + d, NY) * NX + x) * NC + c, z)

    partner = ((y * NX + x) * NC + (1 - c), z)

    peers = [at_z(1), at_z(NZ - 1)]
    peers += [at_x(1), at_x(NX - 1), at_y(1), at_y(NY - 1), partner]
    barrier = pltpu.get_barrier_semaphore()
    for p in peers:
        pl.semaphore_signal(barrier, inc=1, device_id=p, device_id_type=MESH)

    cp_w3 = pltpu.make_async_copy(w3_hbm, w3, lsem.at[0])
    cp_w3.start()
    cp_wo = [
        pltpu.make_async_copy(
            wo_hbm.at[:, :, :, pl.ds(q * 1024, 1024)], wo.at[q, z], lsem.at[1 + q]
        )
        for q in range(NC)
    ]
    for cp in cp_wo:
        cp.start()

    for j in range(2):
        t = tok_ref[j * C : (j + 1) * C, :].astype(F32)
        ms = jnp.mean(t * t, -1, keepdims=True)
        g[z, j] = (t * lax.rsqrt(ms + EPS)).astype(BF16)

    def remote(src, dst, ssem, rsem, dev):
        return pltpu.make_async_remote_copy(
            src_ref=src, dst_ref=dst, send_sem=ssem, recv_sem=rsem,
            device_id=dev, device_id_type=MESH,
        )

    def right(i):
        o = lax.rem(z + NZ - i // 2, NZ)
        ref = g.at[o, lax.rem(i, 2)]
        return remote(ref, ref, agr_s.at[i], agr_r.at[i], at_z(1))

    def left(i):
        o = lax.rem(z + i // 2, NZ)
        ref = g.at[o, jnp.where(i == 6, 1, lax.rem(i, 2))]
        return remote(ref, ref, agl_s.at[i], agl_r.at[i], at_z(NZ - 1))

    def wslice(way, k):
        return lax.rem(z + NZ - 1 - k, NZ) if way == 0 else lax.rem(z + 1 + k, NZ)

    def wzr(k):
        ref = wo.at[c, lax.rem(z + NZ - k, NZ), y, x]
        return remote(ref, ref, wzr_s.at[k], wzr_r.at[k], at_z(1))

    def wzl(k):
        ref = wo.at[c, lax.rem(z + k, NZ), y, x]
        return remote(ref, ref, wzl_s.at[k], wzl_r.at[k], at_z(NZ - 1))

    def w1(way, k, d):
        ref = wo.at[c, wslice(way, k), y, x]
        n = way * 12 + k * 3 + d - 1
        dev = at_x(d) if way == 0 else at_y(d)
        return remote(ref, ref, w1_s.at[n], w1_r.at[n], dev)

    def w2(way, k, d):
        o = wslice(way, k)
        ref = wo.at[c, o, y] if way == 0 else wo.at[c, o, :, x]
        n = way * 12 + k * 3 + d - 1
        dev = at_y(d) if way == 0 else at_x(d)
        return remote(ref, ref, w2_s.at[n], w2_r.at[n], dev)

    def wcore(way, k):
        ref = wo.at[c, wslice(way, k)]
        n = way * 4 + k
        return remote(ref, ref, wc_s.at[n], wc_r.at[n], partner)

    ways = (0, 1)

    def start_w1(k, some=ways):
        for way in some:
            for d in range(1, NX):
                w1(way, k, d).start()

    def next_w2(k, some=ways):
        for way in some:
            for d in range(1, NX):
                w1(way, k, d).wait_recv()
            for d in range(1, NX):
                w2(way, k, d).start()

    def next_core(k, some=ways):
        for way in some:
            for d in range(1, NX):
                w2(way, k, d).wait_recv()
            wcore(way, k).start()

    pl.semaphore_wait(barrier, len(peers))
    first = jnp.int32(0)
    right(first).start()
    left(first).start()
    for cp in cp_wo:
        cp.wait()
    wzr(0).start()
    wzl(0).start()
    right(first + 1).start()
    left(first + 1).start()
    for dev in (at_x(NX - 1), at_y(NY - 1)):
        pl.semaphore_signal(hello, inc=1, device_id=dev, device_id_type=MESH)
    wbt[...] = jnp.concatenate(
        [wb_ref[...].astype(F32), jnp.zeros((DK - 2, D), F32)], 0
    ).T.astype(BF16)
    cp_w3.wait()

    ri = lax.broadcasted_iota(jnp.int32, (DK, DK), 0)
    ci = lax.broadcasted_iota(jnp.int32, (DK, DK), 1)
    same = (ri // C) == (ci // C)
    strict = same & (ri > ci)
    lower = same & (ri >= ci)
    eye = jnp.where(ri == ci, 1.0, 0.0).astype(F32)

    tile8 = (ri // 8) == (ci // 8)

    def unit(v):
        return v * lax.rsqrt(jnp.sum(v * v, -1, keepdims=True) + EPS)

    def silu(v):
        return v / (1.0 + jnp.exp(-v))

    def joint(pieces):
        rows = jnp.concatenate([g[o, j] for o, j in pieces], 0)
        proj = [
            jnp.dot(rows, w3[p], preferred_element_type=F32) for p in range(3)
        ]
        pre = jnp.dot(rows, wbt[...], preferred_element_type=F32)
        qs = silu(proj[0])
        ks = silu(proj[1])
        vs = silu(proj[2])
        qh = [unit(qs[:, h * DK : (h + 1) * DK]) for h in range(2)]
        kh = [unit(ks[:, h * DK : (h + 1) * DK]) for h in range(2)]
        vh = [vs[:, h * DK : (h + 1) * DK] for h in range(2)]
        bh = [
            1.0 / (1.0 + jnp.exp(-(jnp.broadcast_to(pre[:, h : h + 1], (DK, DK)) + bias_ref[h])))
            for h in range(2)
        ]
        def both(f, *lists):
            return [f(*args) for args in zip(*lists)]

        def stack(v):
            return [
                jnp.concatenate([v[0][a * C : (a + 1) * C], v[1][a * C : (a + 1) * C]], 0)
                for a in range(2)
            ]

        q, k, v, b = stack(qh), stack(kh), stack(vh), stack(bh)
        gram = both(lambda m: dot3(m, m, NT), k)
        low = both(lambda m, n: jnp.where(strict, m * n, 0.0), gram, b)
        near = both(lambda m: jnp.where(tile8, m, 0.0), low)
        off = both(lambda m: jnp.where(tile8, 0.0, m), low)
        rhs = both(lambda bb, kk, vv: jnp.concatenate([bb * kk, bb * vv], 1), b, k, v)
        near2 = both(dot3, near, near)
        part = both(lambda m, m2: eye - m + dot3(eye - m, m2), near, near2)
        near4 = both(dot3, near2, near2)
        masked = both(lambda m, n: jnp.where(lower, dot1(m, n, NT), 0.0), q, k)
        inv8 = both(lambda m, m4: m + dot3(m, m4), part, near4)
        step1 = both(dot3, inv8, off)
        wu = both(dot3, inv8, rhs)
        step2 = both(dot3, step1, step1)
        wu = both(lambda m, r: r - dot3(m, r), step1, wu)
        step4 = both(dot3, step2, step2)
        wu = both(lambda m, r: r + dot3(m, r), step2, wu)
        wu = both(lambda m, r: r + dot3(m, r), step4, wu)
        mwu = both(dot1, masked, wu)
        pairs = []
        for a in range(2):
            for h in range(2):
                hp = slice(h * C, (h + 1) * C)
                pairs.append(dot3(wu[a][hp], k[a][hp], TN))
        for a, (o, j) in enumerate(pieces):
            blk = 2 * o + j
            for h in range(2):
                hp = slice(h * C, (h + 1) * C)
                pair = pairs[2 * a + h]
                qe[h, blk] = q[a][hp] - mwu[a][hp, :DK]
                mu[h, blk] = mwu[a][hp, DK:]
                db[h, blk, :DK] = -pair[:DK]
                db[h, blk, DK:] = pair[DK:]

    last = lax.rem(z + NZ // 2, NZ)
    zero = jnp.zeros((2 * DK, DK), F32)

    def fold_second(o, h):
        q = qe[h, 2 * o + 1]
        both = dot1(q, db[h, 2 * o], NT)
        qe[h, 2 * o + 1] = q + both[:, :DK]
        mu[h, 2 * o + 1] = mu[h, 2 * o + 1] + both[:, DK:]

    def close_chunk(o):
        for h in range(2):
            fold_second(o, h)
            ct[h, o] = compose(db[h, 2 * o], db[h, 2 * o + 1])

    def run_chain(o, carry):
        nxt = []
        for h in range(2):
            here = ct[h, o]
            ct[h, o] = carry[h]
            nxt.append(compose(carry[h], here))
        return tuple(nxt)

    def work(oa, ja, ob, jb, closing):
        joint([(oa, ja), (ob, jb)])

        def close(n, carry):
            close_chunk(jnp.where(n == 0, oa, ob))
            return carry

        lax.fori_loop(0, closing, close, 0)

    work(z, 0, z, 1, 1)
    pl.semaphore_wait(hello, 2)

    def step(t, carry):
        i = t - 1
        mid = t <= 6
        even = lax.rem(t, 2) == 0

        @pl.when(t == 7)
        def _():
            wzr(3).wait_recv()
            start_w1(3, (0,))
            for n, (lo, hi) in enumerate(((0, last), (last + 1, NZ))):
                got = lax.fori_loop(lo, hi, run_chain, (zero, zero))
                for h in range(2):
                    ends[n, h] = got[h]

        early = jnp.logical_and(jnp.logical_not(even), mid)

        @pl.when(early)
        def _():
            k = i // 2
            wzr(k).wait_recv()
            wzr(k + 1).start()
            wzl(k).wait_recv()

            @pl.when(k <= 1)
            def _():
                wzl(k + 1).start()

        right(i).wait_recv()

        @pl.when(i <= 4)
        def _():
            right(i + 2).start()

        left(i).wait_recv()

        @pl.when(i <= 3)
        def _():
            left(i + 2).start()

        @pl.when(i == 5)
        def _():
            left(i + 1).start()

        @pl.when(early)
        def _():
            start_w1(i // 2)

        @pl.when(even)
        def _():
            next_w2(t // 2 - 1)

            @pl.when(t >= 4)
            def _():
                next_core(t // 2 - 2)

        @pl.when(t == 7)
        def _():
            next_w2(3, (0,))

        hop = (i + 2) // 2
        ja = jnp.where(mid, lax.rem(i, 2), 0)
        jb = jnp.where(mid, lax.rem(i, 2), 1)
        oa = lax.rem(z + NZ - hop, NZ)
        ob = lax.rem(z + hop, NZ)
        work(oa, ja, ob, jb, jnp.where(jnp.logical_and(mid, even), 2, 0))
        return carry

    lax.fori_loop(1, 8, step, 0)

    head = [compose(ends[0, h], db[h, 2 * last]) for h in range(2)]
    rest = [compose(db[h, 2 * last + 1], ends[1, h]) for h in range(2)]
    for h in range(2):
        tot[h] = compose(head[h], rest[h])

    def core_swap():
        return remote(tot.at[1 - c], lv.at[c], sc_s.at[0], sc_r.at[0], partner)

    core_swap().start()
    lv[c] = tot[c]

    def fold_queries(first, final):
        def one(o, carry):
            after = jnp.broadcast_to((o > last).astype(jnp.int32), (2 * DK, DK)) > 0
            for h in range(2):
                m = compose(jnp.where(after, ends[0, h], 0.0), ct[h, o])
                q = jnp.concatenate([qe[h, 2 * o], qe[h, 2 * o + 1]], 0)
                both = dot1(q, m, NT)
                new = q + both[:, :DK]
                qe[h, 2 * o] = new[:C]
                qe[h, 2 * o + 1] = new[C:]
                mu[h, 2 * o] = mu[h, 2 * o] + both[:C, DK:]
                mu[h, 2 * o + 1] = mu[h, 2 * o + 1] + both[C:, DK:]
            return carry

        lax.fori_loop(first, final, one, 0)

    for h in range(2):
        ct[h, last] = ends[0, h]
        ends[0, h] = compose(head[h], db[h, 2 * last + 1])
        fold_second(last, h)
    core_swap().wait_recv()

    group = compose(lv[0], lv[1])
    sends = []
    xs[0] = group.astype(BF16)
    for d in range(1, NX):
        cp = remote(xs.at[0], xg.at[x], sc_s.at[d], sc_r.at[d], at_x(d))
        cp.start()
        sends.append(cp)
    xg[x] = group.astype(BF16)
    fold_queries(0, 4)
    for d in range(1, NX):
        sends[d - 1].wait_recv()
    part = [xg[n].astype(F32) for n in range(NX)]
    p01 = compose(part[0], part[1])
    p23 = compose(part[2], part[3])
    p012 = compose(p01, part[2])
    group = compose(p01, p23)
    xv = jnp.broadcast_to(x, (2 * DK, DK))
    before = jnp.where(xv == 1, part[0], 0.0)
    before = jnp.where(xv == 2, p01, before)
    before = jnp.where(xv == 3, p012, before)

    yp = jnp.where(lax.rem(y, 2) == 0, 1, NY - 1)
    yq = lax.rem(2 * NY - 1 - 2 * y, NY)
    xs[1] = group.astype(BF16)
    cp = remote(xs.at[1], xr, sc_s.at[7], sc_r.at[7], at_y(yp))
    cp.start()
    sends.append(cp)
    next_core(2)
    fold_queries(4, 6)
    cp.wait_recv()
    other = xr[...].astype(F32)
    low = jnp.broadcast_to(lax.rem(y, 2), (2 * DK, DK)) == 0
    group = compose(jnp.where(low, group, other), jnp.where(low, other, group))
    before = jnp.where(low, before, compose(other, before))

    ys[...] = group[DK:].astype(BF16)
    far = at_y(yq)
    for q in range(NC):
        dev = (far[0] - c + q, z)
        cp = remote(ys, yr.at[c], sc_s.at[4 + q], sc_r.at[4 + c], dev)
        cp.start()
        sends.append(cp)

    def got_y(h):
        return remote(ys, yr.at[h], sc_s.at[4 + h], sc_r.at[4 + h], partner)

    before1 = compose(before, lv[0])
    zero_core = jnp.broadcast_to(c, (2 * DK, DK)) == 0
    es[...] = jnp.where(zero_core, before1, before)
    give = remote(es, eb.at[c], sc_s.at[6], sc_r.at[6], partner)
    give.start()
    eb[c] = jnp.where(zero_core, before, before1)
    next_core(3, (0,))
    fold_queries(6, 8)
    give.wait_recv()
    high = jnp.broadcast_to((y >= 2).astype(jnp.int32), (DK, DK)) > 0
    sin = []
    for h in range(2):
        got_y(h).wait_recv()
        base = jnp.where(high, yr[h].astype(F32), 0.0)
        sin.append(base + dot3(base, eb[h, :DK]) + eb[h, DK:])
    for h in range(2):
        sf[h] = sin[h]

    def a2a(d, o):
        return remote(osend.at[o], fbuf.at[z], a2_s.at[d - 1], a2_r.at[d - 1], (s, o))

    def emit(i, carry):
        d = jnp.where(lax.rem(i, 2) == 1, 4 - (i + 1) // 2, 4 + i // 2)
        o = lax.rem(z + d, NZ)
        cols = []
        for h in range(2):
            q = jnp.concatenate([qe[h, 2 * o], qe[h, 2 * o + 1]], 0)
            m = jnp.concatenate([mu[h, 2 * o], mu[h, 2 * o + 1]], 0)
            full = m + dot1(q, sf[h], NT)
            ms = jnp.mean(full * full, -1, keepdims=True)
            cols.append((full * lax.rsqrt(ms + EPS)).astype(BF16))
        rows = jnp.concatenate(cols, 1)

        @pl.when(i < 7)
        def _():
            osend[o] = rows
            a2a(d, o).start()

        @pl.when(i == 7)
        def _():
            fbuf[z] = rows

        return carry

    lax.fori_loop(0, NZ, emit, 0)

    for k in range(4):
        wcore(0, k).wait_recv()
        if k < 3:
            wcore(1, k).wait_recv()

    def finish(i, carry):
        n = i - 1
        d = jnp.where(lax.rem(n, 2) == 1, 4 - (n + 1) // 2, 4 + n // 2)
        d = jnp.where(i == 0, 0, d)
        src = lax.rem(z + NZ - d, NZ)

        @pl.when(i >= 1)
        def _():
            remote(
                osend.at[src], fbuf.at[src], a2_s.at[d - 1], a2_r.at[d - 1], (s, src)
            ).wait_recv()

        rows = fbuf[src]
        for half in range(2):
            w = wo[half, src].reshape(2 * DK, 1024)
            term = jnp.dot(rows, w, preferred_element_type=F32)
            cols = slice(half * 1024, (half + 1) * 1024)

            @pl.when(i == 0)
            def _():
                acc[:, cols] = term

            @pl.when(i >= 1)
            def _():
                acc[:, cols] = acc[:, cols] + term

        return carry

    lax.fori_loop(0, NZ, finish, 0)
    out_ref[...] = acc[...].astype(BF16)

    for i in range(7):
        right(jnp.int32(i)).wait_send()
        left(jnp.int32(i)).wait_send()
    for d in range(1, NZ):
        a2a(d, lax.rem(z + d, NZ)).wait_send()
    for k in range(4):
        wzr(k).wait_send()
        for way in ways[: 2 if k < 3 else 1]:
            wcore(way, k).wait_send()
            for d in range(1, NX):
                w1(way, k, d).wait_send()
                w2(way, k, d).wait_send()
        if k < 3:
            wzl(k).wait_send()
    core_swap().wait_send()
    for cp in sends:
        cp.wait_send()
    give.wait_send()


def body(tokens, w_qkv, w_beta, beta_bias, w_out):
    w3 = jnp.transpose(w_qkv, (1, 0, 2))
    wb = jnp.transpose(w_beta, (1, 0))
    wo = w_out.reshape(NY, NX, 16, D)
    vmem = pl.BlockSpec(memory_space=pltpu.VMEM)
    hbm = pl.BlockSpec(memory_space=pl.ANY)
    smem = pl.BlockSpec(memory_space=pltpu.SMEM)
    dma = pltpu.SemaphoreType.DMA
    return pl.pallas_call(
        kernel,
        out_shape=jax.ShapeDtypeStruct((2 * C, D), BF16),
        in_specs=[vmem, hbm, vmem, smem, hbm],
        out_specs=vmem,
        scratch_shapes=[
            pltpu.VMEM((NZ, 2, C, D), BF16),
            pltpu.VMEM((3, D, 2 * DK), BF16),
            pltpu.VMEM((D, DK), BF16),
            pltpu.VMEM((2, NZ, NY, NX, 16, 1024), BF16),
            pltpu.VMEM((2, 16, C, DK), F32),
            pltpu.VMEM((2, 16, C, DK), F32),
            pltpu.VMEM((2, 16, 2 * DK, DK), F32),
            pltpu.VMEM((2, NZ, 2 * DK, DK), F32),
            pltpu.VMEM((2, 2, 2 * DK, DK), F32),
            pltpu.VMEM((2, 2 * DK, DK), F32),
            pltpu.VMEM((2, 2 * DK, DK), F32),
            pltpu.VMEM((2, 2 * DK, DK), BF16),
            pltpu.VMEM((2 * DK, DK), BF16),
            pltpu.VMEM((NX, 2 * DK, DK), BF16),
            pltpu.VMEM((DK, DK), BF16),
            pltpu.VMEM((2, DK, DK), BF16),
            pltpu.VMEM((2, 2 * DK, DK), F32),
            pltpu.VMEM((2 * DK, DK), F32),
            pltpu.VMEM((2, DK, DK), F32),
            pltpu.VMEM((NZ, 2 * C, 2 * DK), BF16),
            pltpu.VMEM((NZ, 2 * C, 2 * DK), BF16),
            pltpu.VMEM((2 * C, D), F32),
            pltpu.SemaphoreType.REGULAR,
            dma((3,)),
            dma((7,)),
            dma((7,)),
            dma((7,)),
            dma((7,)),
            dma((4,)),
            dma((4,)),
            dma((3,)),
            dma((3,)),
            dma((21,)),
            dma((21,)),
            dma((21,)),
            dma((21,)),
            dma((7,)),
            dma((7,)),
            dma((8,)),
            dma((8,)),
            dma((7,)),
            dma((7,)),
        ],
        compiler_params=pltpu.CompilerParams(
            collective_id=0, has_side_effects=True, vmem_limit_bytes=60 * 1024 * 1024
        ),
        name="delta_layer",
    )(tokens, w3, wb, beta_bias, wo)


def solution(mesh):
    return jax.shard_map(
        body,
        mesh=mesh,
        in_specs=(
            P(("seq", "head"), None),
            P(None, None, "head"),
            P(None, "head"),
            P("head"),
            P("head", None),
        ),
        out_specs=P(("seq", "head"), None),
        check_vma=False,
    )
```

```python
import jax
import jax.numpy as jnp
from jax import lax
from jax.experimental import pallas as pl
from jax.experimental.pallas import tpu as pltpu
from jax.sharding import PartitionSpec as P

F32 = jnp.float32
BF16 = jnp.bfloat16
MESH = pl.DeviceIdType.MESH
EPS = 1e-6
NZ = 8
NX = 4
NY = 4
NC = 2
C = 64
DK = 128
D = 2048

NN = (((1,), (0,)), ((), ()))
NT = (((1,), (1,)), ((), ()))
TN = (((0,), (0,)), ((), ()))


def halves(a):
    hi = a.astype(BF16)
    lo = (a - hi.astype(F32)).astype(BF16)
    return hi, lo


def dot3(a, b, dims=NN):
    ca = dims[0][0][0]
    cb = dims[0][1][0]
    ah, al = halves(a)
    bh, bl = halves(b)
    return lax.dot_general(
        jnp.concatenate([ah, al, ah], ca),
        jnp.concatenate([bh, bh, bl], cb),
        dims,
        preferred_element_type=F32,
    )


def dot1(a, b, dims=NN):
    return lax.dot_general(
        a.astype(BF16), b.astype(BF16), dims, preferred_element_type=F32
    )


def compose(first, second):
    return first + dot3(first, second[:DK]) + second


def kernel(
    tok_ref,
    w3_hbm,
    wb_ref,
    bias_ref,
    wo_hbm,
    out_ref,
    g,
    w3,
    wbt,
    wo,
    qe,
    mu,
    db,
    ct,
    ends,
    tot,
    lv,
    xs,
    xr,
    xg,
    ys,
    yr,
    eb,
    es,
    sf,
    osend,
    fbuf,
    acc,
    hello,
    lsem,
    agr_s,
    agr_r,
    agl_s,
    agl_r,
    wzr_s,
    wzr_r,
    wzl_s,
    wzl_r,
    w1_s,
    w1_r,
    w2_s,
    w2_r,
    wc_s,
    wc_r,
    sc_s,
    sc_r,
    a2_s,
    a2_r,
):
    s = lax.axis_index("seq")
    z = lax.axis_index("head")
    c = lax.rem(s, NC)
    x = lax.rem(s // NC, NX)
    y = s // (NC * NX)

    def at_z(d):
        return (s, lax.rem(z + d, NZ))

    def at_x(d):
        return ((y * NX + lax.rem(x + d, NX)) * NC + c, z)

    def at_y(d):
        return ((lax.rem(y + d, NY) * NX + x) * NC + c, z)

    partner = ((y * NX + x) * NC + (1 - c), z)

    peers = [at_z(1), at_z(NZ - 1)]
    peers += [at_x(1), at_x(NX - 1), at_y(1), at_y(NY - 1), partner]
    barrier = pltpu.get_barrier_semaphore()
    for p in peers:
        pl.semaphore_signal(barrier, inc=1, device_id=p, device_id_type=MESH)

    cp_w3 = pltpu.make_async_copy(w3_hbm, w3, lsem.at[0])
    cp_w3.start()
    cp_wo = [
        pltpu.make_async_copy(
            wo_hbm.at[:, :, :, pl.ds(q * 1024, 1024)], wo.at[q, z], lsem.at[1 + q]
        )
        for q in range(NC)
    ]
    for cp in cp_wo:
        cp.start()

    for j in range(2):
        t = tok_ref[j * C : (j + 1) * C, :].astype(F32)
        ms = jnp.mean(t * t, -1, keepdims=True)
        g[z, j] = (t * lax.rsqrt(ms + EPS)).astype(BF16)

    def remote(src, dst, ssem, rsem, dev):
        return pltpu.make_async_remote_copy(
            src_ref=src, dst_ref=dst, send_sem=ssem, recv_sem=rsem,
            device_id=dev, device_id_type=MESH,
        )

    def right(i):
        o = lax.rem(z + NZ - i // 2, NZ)
        ref = g.at[o, lax.rem(i, 2)]
        return remote(ref, ref, agr_s.at[i], agr_r.at[i], at_z(1))

    def left(i):
        o = lax.rem(z + i // 2, NZ)
        ref = g.at[o, jnp.where(i == 6, 1, lax.rem(i, 2))]
        return remote(ref, ref, agl_s.at[i], agl_r.at[i], at_z(NZ - 1))

    def wslice(way, k):
        return lax.rem(z + NZ - 1 - k, NZ) if way == 0 else lax.rem(z + 1 + k, NZ)

    def wzr(k):
        ref = wo.at[c, lax.rem(z + NZ - k, NZ), y, x]
        return remote(ref, ref, wzr_s.at[k], wzr_r.at[k], at_z(1))

    def wzl(k):
        ref = wo.at[c, lax.rem(z + k, NZ), y, x]
        return remote(ref, ref, wzl_s.at[k], wzl_r.at[k], at_z(NZ - 1))

    def w1(way, k, d):
        ref = wo.at[c, wslice(way, k), y, x]
        n = way * 12 + k * 3 + d - 1
        dev = at_x(d) if way == 0 else at_y(d)
        return remote(ref, ref, w1_s.at[n], w1_r.at[n], dev)

    def w2(way, k, d):
        o = wslice(way, k)
        ref = wo.at[c, o, y] if way == 0 else wo.at[c, o, :, x]
        n = way * 12 + k * 3 + d - 1
        dev = at_y(d) if way == 0 else at_x(d)
        return remote(ref, ref, w2_s.at[n], w2_r.at[n], dev)

    def wcore(way, k):
        ref = wo.at[c, wslice(way, k)]
        n = way * 4 + k
        return remote(ref, ref, wc_s.at[n], wc_r.at[n], partner)

    ways = (0, 1)

    def start_w1(k, some=ways):
        for way in some:
            for d in range(1, NX):
                w1(way, k, d).start()

    def next_w2(k, some=ways):
        for way in some:
            for d in range(1, NX):
                w1(way, k, d).wait_recv()
            for d in range(1, NX):
                w2(way, k, d).start()

    def next_core(k, some=ways):
        for way in some:
            for d in range(1, NX):
                w2(way, k, d).wait_recv()
            wcore(way, k).start()

    pl.semaphore_wait(barrier, len(peers))
    first = jnp.int32(0)
    right(first).start()
    left(first).start()
    for cp in cp_wo:
        cp.wait()
    wzr(0).start()
    wzl(0).start()
    right(first + 1).start()
    left(first + 1).start()
    for dev in (at_x(NX - 1), at_y(NY - 1)):
        pl.semaphore_signal(hello, inc=1, device_id=dev, device_id_type=MESH)
    wbt[...] = jnp.concatenate(
        [wb_ref[...].astype(F32), jnp.zeros((DK - 2, D), F32)], 0
    ).T.astype(BF16)
    cp_w3.wait()

    ri = lax.broadcasted_iota(jnp.int32, (DK, DK), 0)
    ci = lax.broadcasted_iota(jnp.int32, (DK, DK), 1)
    same = (ri // C) == (ci // C)
    strict = same & (ri > ci)
    lower = same & (ri >= ci)
    eye = jnp.where(ri == ci, 1.0, 0.0).astype(F32)

    tile8 = (ri // 8) == (ci // 8)

    def unit(v):
        return v * lax.rsqrt(jnp.sum(v * v, -1, keepdims=True) + EPS)

    def silu(v):
        return v / (1.0 + jnp.exp(-v))

    def joint(pieces):
        rows = jnp.concatenate([g[o, j] for o, j in pieces], 0)
        proj = [
            jnp.dot(rows, w3[p], preferred_element_type=F32) for p in range(3)
        ]
        pre = jnp.dot(rows, wbt[...], preferred_element_type=F32)
        qs = silu(proj[0])
        ks = silu(proj[1])
        vs = silu(proj[2])
        qh = [unit(qs[:, h * DK : (h + 1) * DK]) for h in range(2)]
        kh = [unit(ks[:, h * DK : (h + 1) * DK]) for h in range(2)]
        vh = [vs[:, h * DK : (h + 1) * DK] for h in range(2)]
        bh = [
            1.0 / (1.0 + jnp.exp(-(jnp.broadcast_to(pre[:, h : h + 1], (DK, DK)) + bias_ref[h])))
            for h in range(2)
        ]
        def both(f, *lists):
            return [f(*args) for args in zip(*lists)]

        def stack(v):
            return [
                jnp.concatenate([v[0][a * C : (a + 1) * C], v[1][a * C : (a + 1) * C]], 0)
                for a in range(2)
            ]

        q, k, v, b = stack(qh), stack(kh), stack(vh), stack(bh)
        gram = both(lambda m: dot3(m, m, NT), k)
        low = both(lambda m, n: jnp.where(strict, m * n, 0.0), gram, b)
        near = both(lambda m: jnp.where(tile8, m, 0.0), low)
        off = both(lambda m: jnp.where(tile8, 0.0, m), low)
        rhs = both(lambda bb, kk, vv: jnp.concatenate([bb * kk, bb * vv], 1), b, k, v)
        near2 = both(dot3, near, near)
        part = both(lambda m, m2: eye - m + dot3(eye - m, m2), near, near2)
        near4 = both(dot3, near2, near2)
        masked = both(lambda m, n: jnp.where(lower, dot1(m, n, NT), 0.0), q, k)
        inv8 = both(lambda m, m4: m + dot3(m, m4), part, near4)
        step1 = both(dot3, inv8, off)
        wu = both(dot3, inv8, rhs)
        step2 = both(dot3, step1, step1)
        wu = both(lambda m, r: r - dot3(m, r), step1, wu)
        step4 = both(dot3, step2, step2)
        wu = both(lambda m, r: r + dot3(m, r), step2, wu)
        wu = both(lambda m, r: r + dot3(m, r), step4, wu)
        mwu = both(dot1, masked, wu)
        pairs = []
        for a in range(2):
            for h in range(2):
                hp = slice(h * C, (h + 1) * C)
                pairs.append(dot3(wu[a][hp], k[a][hp], TN))
        for a, (o, j) in enumerate(pieces):
            blk = 2 * o + j
            for h in range(2):
                hp = slice(h * C, (h + 1) * C)
                pair = pairs[2 * a + h]
                qe[h, blk] = q[a][hp] - mwu[a][hp, :DK]
                mu[h, blk] = mwu[a][hp, DK:]
                db[h, blk, :DK] = -pair[:DK]
                db[h, blk, DK:] = pair[DK:]

    last = lax.rem(z + NZ // 2, NZ)
    zero = jnp.zeros((2 * DK, DK), F32)

    def fold_second(o, h):
        q = qe[h, 2 * o + 1]
        both = dot1(q, db[h, 2 * o], NT)
        qe[h, 2 * o + 1] = q + both[:, :DK]
        mu[h, 2 * o + 1] = mu[h, 2 * o + 1] + both[:, DK:]

    def close_chunk(o):
        for h in range(2):
            fold_second(o, h)
            ct[h, o] = compose(db[h, 2 * o], db[h, 2 * o + 1])

    def run_chain(o, carry):
        nxt = []
        for h in range(2):
            here = ct[h, o]
            ct[h, o] = carry[h]
            nxt.append(compose(carry[h], here))
        return tuple(nxt)

    def work(oa, ja, ob, jb, closing):
        joint([(oa, ja), (ob, jb)])

        def close(n, carry):
            close_chunk(jnp.where(n == 0, oa, ob))
            return carry

        lax.fori_loop(0, closing, close, 0)

    work(z, 0, z, 1, 1)
    pl.semaphore_wait(hello, 2)

    def step(t, carry):
        i = t - 1
        mid = t <= 6
        even = lax.rem(t, 2) == 0

        @pl.when(t == 7)
        def _():
            wzr(3).wait_recv()
            start_w1(3, (0,))
            for n, (lo, hi) in enumerate(((0, last), (last + 1, NZ))):
                got = lax.fori_loop(lo, hi, run_chain, (zero, zero))
                for h in range(2):
                    ends[n, h] = got[h]

        early = jnp.logical_and(jnp.logical_not(even), mid)

        @pl.when(early)
        def _():
            k = i // 2
            wzr(k).wait_recv()
            wzr(k + 1).start()
            wzl(k).wait_recv()

            @pl.when(k <= 1)
            def _():
                wzl(k + 1).start()

        right(i).wait_recv()

        @pl.when(i <= 4)
        def _():
            right(i + 2).start()

        left(i).wait_recv()

        @pl.when(i <= 3)
        def _():
            left(i + 2).start()

        @pl.when(i == 5)
        def _():
            left(i + 1).start()

        @pl.when(early)
        def _():
            start_w1(i // 2)

        @pl.when(even)
        def _():
            next_w2(t // 2 - 1)

            @pl.when(t >= 4)
            def _():
                next_core(t // 2 - 2)

        @pl.when(t == 7)
        def _():
            next_w2(3, (0,))

        hop = (i + 2) // 2
        ja = jnp.where(mid, lax.rem(i, 2), 0)
        jb = jnp.where(mid, lax.rem(i, 2), 1)
        oa = lax.rem(z + NZ - hop, NZ)
        ob = lax.rem(z + hop, NZ)
        work(oa, ja, ob, jb, jnp.where(jnp.logical_and(mid, even), 2, 0))
        return carry

    lax.fori_loop(1, 8, step, 0)

    head = [compose(ends[0, h], db[h, 2 * last]) for h in range(2)]
    rest = [compose(db[h, 2 * last + 1], ends[1, h]) for h in range(2)]
    for h in range(2):
        tot[h] = compose(head[h], rest[h])

    def core_swap():
        return remote(tot.at[1 - c], lv.at[c], sc_s.at[0], sc_r.at[0], partner)

    core_swap().start()
    lv[c] = tot[c]

    def fold_queries(first, final):
        def one(o, carry):
            after = jnp.broadcast_to((o > last).astype(jnp.int32), (2 * DK, DK)) > 0
            for h in range(2):
                m = compose(jnp.where(after, ends[0, h], 0.0), ct[h, o])
                q = jnp.concatenate([qe[h, 2 * o], qe[h, 2 * o + 1]], 0)
                both = dot1(q, m, NT)
                new = q + both[:, :DK]
                qe[h, 2 * o] = new[:C]
                qe[h, 2 * o + 1] = new[C:]
                mu[h, 2 * o] = mu[h, 2 * o] + both[:C, DK:]
                mu[h, 2 * o + 1] = mu[h, 2 * o + 1] + both[C:, DK:]
            return carry

        lax.fori_loop(first, final, one, 0)

    for h in range(2):
        ct[h, last] = ends[0, h]
        ends[0, h] = compose(head[h], db[h, 2 * last + 1])
        fold_second(last, h)
    core_swap().wait_recv()

    group = compose(lv[0], lv[1])
    sends = []
    xs[0] = group.astype(BF16)
    for d in (2, 1, 3):
        cp = remote(xs.at[0], xg.at[x], sc_s.at[d], sc_r.at[d], at_x(d))
        cp.start()
        sends.append(cp)
    xg[x] = group.astype(BF16)
    fold_queries(0, 4)
    for d in range(1, NX):
        sends[d - 1].wait_recv()
    part = [xg[n].astype(F32) for n in range(NX)]
    p01 = compose(part[0], part[1])
    p23 = compose(part[2], part[3])
    p012 = compose(p01, part[2])
    group = compose(p01, p23)
    xv = jnp.broadcast_to(x, (2 * DK, DK))
    before = jnp.where(xv == 1, part[0], 0.0)
    before = jnp.where(xv == 2, p01, before)
    before = jnp.where(xv == 3, p012, before)

    yp = jnp.where(lax.rem(y, 2) == 0, 1, NY - 1)
    yq = lax.rem(2 * NY - 1 - 2 * y, NY)
    xs[1] = group.astype(BF16)
    cp = remote(xs.at[1], xr, sc_s.at[7], sc_r.at[7], at_y(yp))
    cp.start()
    sends.append(cp)
    next_core(2)
    fold_queries(4, 6)
    cp.wait_recv()
    other = xr[...].astype(F32)
    low = jnp.broadcast_to(lax.rem(y, 2), (2 * DK, DK)) == 0
    group = compose(jnp.where(low, group, other), jnp.where(low, other, group))
    before = jnp.where(low, before, compose(other, before))

    ys[...] = group[DK:].astype(BF16)
    far = at_y(yq)
    for q in range(NC):
        dev = (far[0] - c + q, z)
        cp = remote(ys, yr.at[c], sc_s.at[4 + q], sc_r.at[4 + c], dev)
        cp.start()
        sends.append(cp)

    def got_y(h):
        return remote(ys, yr.at[h], sc_s.at[4 + h], sc_r.at[4 + h], partner)

    before1 = compose(before, lv[0])
    zero_core = jnp.broadcast_to(c, (2 * DK, DK)) == 0
    es[...] = jnp.where(zero_core, before1, before)
    give = remote(es, eb.at[c], sc_s.at[6], sc_r.at[6], partner)
    give.start()
    eb[c] = jnp.where(zero_core, before, before1)
    next_core(3, (0,))
    fold_queries(6, 8)
    give.wait_recv()
    high = jnp.broadcast_to((y >= 2).astype(jnp.int32), (DK, DK)) > 0
    sin = []
    for h in range(2):
        got_y(h).wait_recv()
        base = jnp.where(high, yr[h].astype(F32), 0.0)
        sin.append(base + dot3(base, eb[h, :DK]) + eb[h, DK:])
    for h in range(2):
        sf[h] = sin[h]

    def a2a(d, o):
        return remote(osend.at[o], fbuf.at[z], a2_s.at[d - 1], a2_r.at[d - 1], (s, o))

    def emit(i, carry):
        d = jnp.where(lax.rem(i, 2) == 1, 4 - (i + 1) // 2, 4 + i // 2)
        o = lax.rem(z + d, NZ)
        cols = []
        for h in range(2):
            q = jnp.concatenate([qe[h, 2 * o], qe[h, 2 * o + 1]], 0)
            m = jnp.concatenate([mu[h, 2 * o], mu[h, 2 * o + 1]], 0)
            full = m + dot1(q, sf[h], NT)
            ms = jnp.mean(full * full, -1, keepdims=True)
            cols.append((full * lax.rsqrt(ms + EPS)).astype(BF16))
        rows = jnp.concatenate(cols, 1)

        @pl.when(i < 7)
        def _():
            osend[o] = rows
            a2a(d, o).start()

        @pl.when(i == 7)
        def _():
            fbuf[z] = rows

        return carry

    lax.fori_loop(0, NZ, emit, 0)

    for k in range(4):
        wcore(0, k).wait_recv()
        if k < 3:
            wcore(1, k).wait_recv()

    def finish(i, carry):
        n = i - 1
        d = jnp.where(lax.rem(n, 2) == 1, 4 - (n + 1) // 2, 4 + n // 2)
        d = jnp.where(i == 0, 0, d)
        src = lax.rem(z + NZ - d, NZ)

        @pl.when(i >= 1)
        def _():
            remote(
                osend.at[src], fbuf.at[src], a2_s.at[d - 1], a2_r.at[d - 1], (s, src)
            ).wait_recv()

        rows = fbuf[src]
        for half in range(2):
            w = wo[half, src].reshape(2 * DK, 1024)
            term = jnp.dot(rows, w, preferred_element_type=F32)
            cols = slice(half * 1024, (half + 1) * 1024)

            @pl.when(i == 0)
            def _():
                acc[:, cols] = term

            @pl.when(i >= 1)
            def _():
                acc[:, cols] = acc[:, cols] + term

        return carry

    lax.fori_loop(0, NZ, finish, 0)
    out_ref[...] = acc[...].astype(BF16)

    for i in range(7):
        right(jnp.int32(i)).wait_send()
        left(jnp.int32(i)).wait_send()
    for d in range(1, NZ):
        a2a(d, lax.rem(z + d, NZ)).wait_send()
    for k in range(4):
        wzr(k).wait_send()
        for way in ways[: 2 if k < 3 else 1]:
            wcore(way, k).wait_send()
            for d in range(1, NX):
                w1(way, k, d).wait_send()
                w2(way, k, d).wait_send()
        if k < 3:
            wzl(k).wait_send()
    core_swap().wait_send()
    for cp in sends:
        cp.wait_send()
    give.wait_send()


def body(tokens, w_qkv, w_beta, beta_bias, w_out):
    w3 = jnp.transpose(w_qkv, (1, 0, 2))
    wb = jnp.transpose(w_beta, (1, 0))
    wo = w_out.reshape(NY, NX, 16, D)
    vmem = pl.BlockSpec(memory_space=pltpu.VMEM)
    hbm = pl.BlockSpec(memory_space=pl.ANY)
    smem = pl.BlockSpec(memory_space=pltpu.SMEM)
    dma = pltpu.SemaphoreType.DMA
    return pl.pallas_call(
        kernel,
        out_shape=jax.ShapeDtypeStruct((2 * C, D), BF16),
        in_specs=[vmem, hbm, vmem, smem, hbm],
        out_specs=vmem,
        scratch_shapes=[
            pltpu.VMEM((NZ, 2, C, D), BF16),
            pltpu.VMEM((3, D, 2 * DK), BF16),
            pltpu.VMEM((D, DK), BF16),
            pltpu.VMEM((2, NZ, NY, NX, 16, 1024), BF16),
            pltpu.VMEM((2, 16, C, DK), F32),
            pltpu.VMEM((2, 16, C, DK), F32),
            pltpu.VMEM((2, 16, 2 * DK, DK), F32),
            pltpu.VMEM((2, NZ, 2 * DK, DK), F32),
            pltpu.VMEM((2, 2, 2 * DK, DK), F32),
            pltpu.VMEM((2, 2 * DK, DK), F32),
            pltpu.VMEM((2, 2 * DK, DK), F32),
            pltpu.VMEM((2, 2 * DK, DK), BF16),
            pltpu.VMEM((2 * DK, DK), BF16),
            pltpu.VMEM((NX, 2 * DK, DK), BF16),
            pltpu.VMEM((DK, DK), BF16),
            pltpu.VMEM((2, DK, DK), BF16),
            pltpu.VMEM((2, 2 * DK, DK), F32),
            pltpu.VMEM((2 * DK, DK), F32),
            pltpu.VMEM((2, DK, DK), F32),
            pltpu.VMEM((NZ, 2 * C, 2 * DK), BF16),
            pltpu.VMEM((NZ, 2 * C, 2 * DK), BF16),
            pltpu.VMEM((2 * C, D), F32),
            pltpu.SemaphoreType.REGULAR,
            dma((3,)),
            dma((7,)),
            dma((7,)),
            dma((7,)),
            dma((7,)),
            dma((4,)),
            dma((4,)),
            dma((3,)),
            dma((3,)),
            dma((21,)),
            dma((21,)),
            dma((21,)),
            dma((21,)),
            dma((7,)),
            dma((7,)),
            dma((8,)),
            dma((8,)),
            dma((7,)),
            dma((7,)),
        ],
        compiler_params=pltpu.CompilerParams(
            collective_id=0, has_side_effects=True, vmem_limit_bytes=60 * 1024 * 1024
        ),
        name="delta_layer",
    )(tokens, w3, wb, beta_bias, wo)


def solution(mesh):
    return jax.shard_map(
        body,
        mesh=mesh,
        in_specs=(
            P(("seq", "head"), None),
            P(None, None, "head"),
            P(None, "head"),
            P("head"),
            P("head", None),
        ),
        out_specs=P(("seq", "head"), None),
        check_vma=False,
    )
```
